32 devices in a mesh: sample: 2 (over y), gx: 16 (over z, x, core).
Axes of the slice: x: 2, y: 2, z: 4, core: 2. Of those that a mesh axis runs over, the one named last changes fastest.
Arguments:
- populations: float32 [19, 32, 128, 256], P(None, ('sample', 'gx')), parts along dimension 1, may hold values from 0.5 to 1.5
- solid_mask: int32 [32, 128, 256], P(('sample', 'gx')), parts along dimension 0, may hold values from 0 to 1, as said below
- relax_rates: float32 [19], replicated, may hold values from 0.7 to 1.9
- body_force: float32 [3], replicated, may hold values from -0.1 to 0.1
Outputs:
- final_populations: float32 [19, 32, 128, 256], P(None, ('sample', 'gx')), parts along dimension 1
The draws below stay inside these ranges and needn't reach their ends.
There are 2 independent parts, one for each index of `sample`. The reference program is written for one: setup_inputs(seed, part) draws one part's arguments, and reference() takes and returns one part's arrays. A program takes and returns all parts, laid end to end along the dimension named above; an argument that names none is the same for every part. Nothing has to cross between parts.
Inputs may be any that keep to these rules, and one draw needn't show every extreme that they name: `solid_mask`: 1 marks a solid node, 0 a fluid node.
All inputs are finite; a program needn't handle non-finite values.
Results may differ from the reference program's by a relative error of at most 0.0003.
Values sent between devices are 32-bit elements; how exact they have to be, the bound alone decides.
No kernel may reach another device: no remote copies, remote signals or barrier semaphores. Data moves between devices by JAX's collectives and lax.ppermute only.
A program may use at most 192 MiB of HBM per device.

```python
import jax
import jax.numpy as jnp
import numpy as np
from jax import lax

NY = 128
NZ = 256
STEPS = 2
NX = 16


def draw_solid_mask(key, part):
    position = lax.broadcasted_iota(jnp.int32, (NX, NY, NZ), 0)
    threshold = 50 + 550 * position // NX
    chance = jax.random.randint(jax.random.fold_in(key, 11), (NX, NY, NZ), 0, 1000)
    return (chance < threshold).astype(jnp.int32)


def levels(key, dims, pieces, smallest, largest):
    gain = 1.0
    for dim, parts in pieces:
        heights = jax.random.uniform(jax.random.fold_in(jax.random.fold_in(key, 6), dim), (parts,), jnp.float32, smallest / len(pieces), largest / len(pieces))
        gain = gain * jnp.repeat(jnp.exp(heights), dims[dim] // parts).reshape((-1,) + (1,) * (len(dims) - 1 - dim))
    return gain


def setup_inputs(seed: int = 0, part: int = 0) -> dict:
    key_of = jax.random.split(jax.random.key(seed), 5)
    part_keys = jax.random.split(jax.random.fold_in(key_of[4], part), 5)
    populations = jnp.clip(0.5 + 1.0 * jax.random.uniform(part_keys[0], (19, NX, NY, NZ), jnp.float32) ** levels(part_keys[0], (19, NX, NY, NZ), ((1, 16),), -0.2, 0.2), 0.5, 1.5)
    solid_mask = draw_solid_mask(jax.random.fold_in(jax.random.fold_in(key_of[4], part), 71), part)
    relax_rates = jnp.clip(jax.random.uniform(key_of[2], (19,), jnp.float32, 0.7, 1.9), 0.7, 1.9)
    body_force = jnp.clip(jax.random.uniform(key_of[3], (3,), jnp.float32, -0.1, 0.1), -0.1, 0.1)
    return {"populations": populations, "solid_mask": solid_mask, "relax_rates": relax_rates, "body_force": body_force}


def lattice_tables():
    velocities = np.array([[0, 0, 0], [1, 0, 0], [-1, 0, 0], [0, 1, 0], [0, -1, 0], [0, 0, 1], [0, 0, -1], [1, 1, 0], [-1, -1, 0], [1, -1, 0], [-1, 1, 0], [1, 0, 1], [-1, 0, -1], [1, 0, -1], [-1, 0, 1], [0, 1, 1], [0, -1, -1], [0, 1, -1], [0, -1, 1]])
    opposite = np.array([0, 2, 1, 4, 3, 6, 5, 8, 7, 10, 9, 12, 11, 14, 13, 16, 15, 18, 17])
    weights = np.array([1.0 / 3.0] + [1.0 / 18.0] * 6 + [1.0 / 36.0] * 12)
    along_x = velocities[:, 0]
    along_y = velocities[:, 1]
    along_z = velocities[:, 2]
    unity = np.ones(19)
    polynomials = np.stack([unity, along_x, along_y, along_z, along_x * along_y, along_x * along_z, along_y * along_z, along_x ** 2, along_y ** 2, along_z ** 2, along_x * along_y ** 2, along_x * along_z ** 2, along_x ** 2 * along_y, along_x ** 2 * along_z, along_y * along_z ** 2, along_y ** 2 * along_z, along_x ** 2 * along_y ** 2, along_x ** 2 * along_z ** 2, along_y ** 2 * along_z ** 2])
    basis = []
    for moment_row in polynomials:
        vector = moment_row.copy()
        for earlier in basis:
            vector = vector - (vector @ earlier) / (earlier @ earlier) * earlier
        basis.append(vector)
    moments = np.stack(basis)
    inverse = moments.T / np.sum(moments ** 2, axis=1)[None, :]
    return velocities, opposite, weights, moments, inverse


def make_kernel(relax_rates, tables):
    inverse = jnp.asarray(tables[4], jnp.float32)
    moments = jnp.asarray(tables[3], jnp.float32)
    return jnp.dot(inverse * relax_rates[None, :], moments, precision=lax.Precision.HIGHEST)


def collide(populations, solid_mask, kernel, body_force, tables):
    lattice_vel = jnp.asarray(tables[0], jnp.float32)
    weight_col = jnp.asarray(tables[2], jnp.float32)[:, None]
    density = jnp.sum(populations, axis=0)
    momentum = jnp.dot(lattice_vel.T, populations, precision=lax.Precision.HIGHEST)
    velocity = momentum / density
    projected = jnp.dot(lattice_vel, velocity, precision=lax.Precision.HIGHEST)
    speed_sq = jnp.sum(velocity * velocity, axis=0)
    equilibrium = weight_col * density * (1.0 + 3.0 * projected + 4.5 * projected * projected - 1.5 * speed_sq)
    relaxed = populations - jnp.dot(kernel, populations - equilibrium, precision=lax.Precision.HIGHEST)
    pushed = 3.0 * jnp.dot(lattice_vel, body_force, precision=lax.Precision.HIGHEST)
    relaxed = relaxed + (weight_col * pushed[:, None]) * density
    reflected = populations[tables[1]]
    return jnp.where(solid_mask[None, :] == 1, reflected, relaxed)


def reference(populations, solid_mask, relax_rates, body_force):
    tables = lattice_tables()
    kernel = make_kernel(relax_rates, tables)
    state = populations

    def one_plane(pair):
        plane, mask_plane = pair
        flat = collide(plane.reshape(19, -1), mask_plane.reshape(-1), kernel, body_force, tables)
        return flat.reshape(plane.shape)

    for step in range(STEPS):
        planes = jnp.moveaxis(state, 1, 0)
        relaxed = jnp.moveaxis(lax.map(one_plane, (planes, solid_mask)), 0, 1)
        moved = []
        for number in range(19):
            offsets = tuple(int(value) for value in tables[0][number])
            moved.append(jnp.roll(relaxed[number], offsets, axis=(0, 1, 2)))
        state = jnp.stack(moved)
    return state
```

```python
import functools

import jax
import jax.numpy as jnp
import numpy as np
from jax import lax
from jax.experimental import pallas as pl
from jax.experimental.pallas import tpu as pltpu
from jax.sharding import PartitionSpec as P

PIECES = 8
LANES = 128
ROWS = 8

UP = (1, 7, 9, 11, 13)
DOWN = (2, 10, 8, 14, 12)
GROUP_SHIFTS = ((0, 0), (1, 0), (-1, 0), (0, 1), (0, -1))
BOUNCE = (0, 2, 1, 4, 3)
FLAT = (0, 3, 4, 5, 6, 15, 16, 17, 18)
FLAT_SHIFTS = ((0, 0), (1, 0), (-1, 0), (0, 1), (0, -1), (1, 1), (-1, -1), (1, -1), (-1, 1))
FLAT_OPPOSITE = (0, 2, 1, 4, 3, 6, 5, 8, 7)


def moment_tables():
    velocities = np.array(
        [
            [0, 0, 0],
            [1, 0, 0],
            [-1, 0, 0],
            [0, 1, 0],
            [0, -1, 0],
            [0, 0, 1],
            [0, 0, -1],
            [1, 1, 0],
            [-1, -1, 0],
            [1, -1, 0],
            [-1, 1, 0],
            [1, 0, 1],
            [-1, 0, -1],
            [1, 0, -1],
            [-1, 0, 1],
            [0, 1, 1],
            [0, -1, -1],
            [0, 1, -1],
            [0, -1, 1],
        ]
    )
    x, y, z = velocities.T
    polynomials = np.stack(
        [
            np.ones(19),
            x,
            y,
            z,
            x * y,
            x * z,
            y * z,
            x**2,
            y**2,
            z**2,
            x * y**2,
            x * z**2,
            x**2 * y,
            x**2 * z,
            y * z**2,
            y**2 * z,
            x**2 * y**2,
            x**2 * z**2,
            y**2 * z**2,
        ]
    ).astype(np.float64)
    basis = []
    for row in polynomials:
        vector = row.copy()
        for earlier in basis:
            vector = vector - vector @ earlier / (earlier @ earlier) * earlier
        basis.append(vector)
    moments = np.stack(basis)
    classes = ((0, 7, 8, 9, 16, 17, 18), (1, 10, 11), (2, 12, 14), (3, 13, 15))
    tables = []
    for numbers in classes:
        rows = list(numbers)
        lower = moments[rows] @ np.linalg.pinv(polynomials[rows])
        lower = np.where(np.abs(lower) < 1e-12, 0.0, lower)
        inverse = np.linalg.inv(lower)
        inverse = np.where(np.abs(inverse) < 1e-12, 0.0, inverse)
        tables.append((numbers, lower, inverse))
    return tables


def relaxing_entries(rates):
    matrices = []
    for numbers, lower, inverse in moment_tables():
        size = len(numbers)
        matrix = {}
        for i in range(size):
            for j in range(i + 1):
                total = None
                for m in range(j, i + 1):
                    factor = float(inverse[i, m] * lower[m, j])
                    if factor == 0.0:
                        continue
                    term = rates[numbers[m]] * factor
                    total = term if total is None else total + term
                if total is not None:
                    matrix[i, j] = total
        matrices.append(matrix)
    return matrices


def apply_lower(matrix, vector):
    out = []
    for i in range(len(vector)):
        total = None
        for j in range(i + 1):
            if (i, j) in matrix:
                term = matrix[i, j] * vector[j]
                total = term if total is None else total + term
        out.append(total)
    return out


def relax(ahead, back, flat, solid, matrices, cross_rates, push):
    axis_sum = (ahead[0] + back[0], flat[1] + flat[2], flat[3] + flat[4])
    axis_odd = (ahead[0] - back[0], flat[1] - flat[2], flat[3] - flat[4])

    def butterfly(pp, pm, mp, mm):
        a, b, c, d = pp + pm, pp - pm, mp + mm, mp - mm
        return a + c, a - c, b + d, b - d

    xy, xy_x, xy_y, xy_xy = butterfly(ahead[1], ahead[2], back[1], back[2])
    xz, xz_x, xz_z, xz_xz = butterfly(ahead[3], ahead[4], back[3], back[4])
    yz, yz_y, yz_z, yz_yz = butterfly(flat[5], flat[7], flat[8], flat[6])
    sx, sy, sz = axis_sum
    density = (flat[0] + (sx + sy)) + ((sz + xy) + (xz + yz))
    jx = axis_odd[0] + (xy_x + xz_x)
    jy = axis_odd[1] + (xy_y + yz_y)
    jz = axis_odd[2] + (xz_z + yz_z)
    over = 1.0 / density
    ux, uy, uz = jx * over, jy * over, jz * over
    qxx, qyy, qzz = jx * ux, jy * uy, jz * uz
    base = (density - 1.5 * (qxx + (qyy + qzz))) * (1.0 / 9.0)
    hx, hy, hz = 0.5 * qxx, 0.5 * qyy, 0.5 * qzz
    bx, by, bz = base + hx, base + hy, base + hz
    rest = flat[0] - 3.0 * base
    sx, sy, sz = sx - bx, sy - by, sz - bz
    xy, xz, yz = xy - (bx + hy), xz - (bx + hz), yz - (by + hz)
    third = 1.0 / 3.0
    tx, ty, tz = jx * third, jy * third, jz * third
    raw = [
        (rest + (sx + sy)) + ((sz + xy) + (xz + yz)),
        sx + (xy + xz),
        sy + (xy + yz),
        sz + (xz + yz),
        xy,
        xz,
        yz,
    ]
    change = apply_lower(matrices[0], raw)
    total, mx, my, mz, cxy, cxz, cyz = change
    even_xy, even_xz, even_yz = 0.25 * cxy, 0.25 * cxz, 0.25 * cyz
    even_x = 0.5 * (mx - (cxy + cxz))
    even_y = 0.5 * (my - (cxy + cyz))
    even_z = 0.5 * (mz - (cxz + cyz))
    even_rest = (total - (mx + my)) + ((cxy + cxz) + (cyz - mz))

    def odd_class(matrix, along, first, second, mean, force):
        first, second = first - mean, second - mean
        along = along - mean
        change = apply_lower(matrix, [along + (first + second), first, second])
        lift = density * force
        return (
            0.5 * ((change[0] - (change[1] + change[2])) - lift),
            0.25 * (change[1] - lift),
            0.25 * (change[2] - lift),
        )

    odd_x, odd_xy_x, odd_xz_x = odd_class(matrices[1], axis_odd[0], xy_x, xz_x, tx, push[0])
    odd_y, odd_xy_y, odd_yz_y = odd_class(matrices[2], axis_odd[1], xy_y, yz_y, ty, push[1])
    odd_z, odd_xz_z, odd_yz_z = odd_class(matrices[3], axis_odd[2], xz_z, yz_z, tz, push[2])
    both_xy = (xy_xy - jx * uy) * cross_rates[0]
    both_xz = (xz_xz - jx * uz) * cross_rates[1]
    both_yz = (yz_yz - jy * uz) * cross_rates[2]

    def spread(even, first, second, both):
        a, b, c, d = even + first, second + both, even - first, second - both
        return a + b, a - b, c + d, c - d

    xy_pp, xy_pm, xy_mp, xy_mm = spread(even_xy, odd_xy_x, odd_xy_y, both_xy)
    xz_pp, xz_pm, xz_mp, xz_mm = spread(even_xz, odd_xz_x, odd_xz_z, both_xz)
    yz_pp, yz_pm, yz_mp, yz_mm = spread(even_yz, odd_yz_y, odd_yz_z, both_yz)
    new_ahead = [even_x + odd_x, xy_pp, xy_pm, xz_pp, xz_pm]
    new_back = [even_x - odd_x, xy_mp, xy_mm, xz_mp, xz_mm]
    new_flat = [
        even_rest,
        even_y + odd_y,
        even_y - odd_y,
        even_z + odd_z,
        even_z - odd_z,
        yz_pp,
        yz_mm,
        yz_pm,
        yz_mp,
    ]
    out_ahead = [
        jnp.where(solid, back[BOUNCE[k]], ahead[k] - new_ahead[k]) for k in range(5)
    ]
    out_back = [jnp.where(solid, ahead[BOUNCE[k]], back[k] - new_back[k]) for k in range(5)]
    out_flat = [
        jnp.where(solid, flat[FLAT_OPPOSITE[k]], flat[k] - new_flat[k]) for k in range(9)
    ]
    return out_ahead, out_back, out_flat


def local_frame():
    return lax.rem(lax.axis_index("gx"), 2)


def select_channel(side, k):
    return jnp.where(side == 1, UP[k], DOWN[k])


def scalars(rates_ref, force_ref, side):
    rates = [rates_ref[m] for m in range(19)]
    third = 1.0 / 3.0
    sign = jnp.where(side == 1, third, -third).astype(jnp.float32)
    push = (force_ref[0] * sign, force_ref[1] * third, force_ref[2] * third)
    scale = 0.25
    cross = tuple(rates[m] * scale for m in (4, 5, 6))
    return relaxing_entries(rates), cross, push


def shifted(ref, channel, shift):
    value = ref[channel]
    if shift[0]:
        value = pltpu.roll(value, shift[0] % value.shape[0], 0)
    if shift[1]:
        value = pltpu.roll(value, shift[1] % value.shape[1], 1)
    return value


def collide_tiles(load, solid_ref, store, first_row, rows, coefficients):
    matrices, cross, push = coefficients

    def body(t, carry):
        row = pl.multiple_of(first_row + t * ROWS, ROWS)
        for lane in range(0, solid_ref.shape[1], LANES):
            where = (pl.ds(row, ROWS), pl.ds(lane, LANES))
            ahead, back, flat = load(where)
            solid = solid_ref[where] == 1
            store(where, *relax(ahead, back, flat, solid, matrices, cross, push))
        return carry

    lax.fori_loop(0, rows // ROWS, body, 0)


def first_kernel(f_ref, mask_ref, rates_ref, force_ref, off_ref, on_ref, flat_ref, f, solid, out, sems):
    height = solid.shape[0]
    rows = height // PIECES
    copies = []
    for piece in range(PIECES):
        part = pl.ds(piece * rows, rows)
        copies.append(
            (
                pltpu.make_async_copy(f_ref.at[:, part, :], f.at[:, part, :], sems.at[0, piece]),
                pltpu.make_async_copy(mask_ref.at[part, :], solid.at[part, :], sems.at[1, piece]),
            )
        )
        for copy in copies[-1]:
            copy.start()
    side = local_frame()
    coefficients = scalars(rates_ref, force_ref, side)
    toward = [select_channel(side, k) for k in range(5)]
    away = [select_channel(1 - side, k) for k in range(5)]

    def load(where):
        return (
            [f[(toward[k], *where)] for k in range(5)],
            [f[(away[k], *where)] for k in range(5)],
            [f[(FLAT[k], *where)] for k in range(9)],
        )

    def store(where, ahead, back, flat):
        for k, value in enumerate(ahead + back + flat):
            out[(k, *where)] = value

    for piece in range(PIECES):
        for copy in copies[piece]:
            copy.wait()
        collide_tiles(load, solid, store, piece * rows, rows, coefficients)
    finish(out, off_ref, on_ref, flat_ref)


def finish(out, off_ref, on_ref, flat_ref):
    for k in range(5):
        off_ref[k] = shifted(out, k, GROUP_SHIFTS[k])
    for k in range(5):
        on_ref[k] = shifted(out, 5 + k, GROUP_SHIFTS[k])
    for k in range(9):
        flat_ref[k] = shifted(out, 10 + k, FLAT_SHIFTS[k])


def second_kernel(
    off_in, on_in, flat_in, mask_ref, rates_ref, force_ref, off_ref, on_ref, out_ref, solid, out, moved, sems
):
    copy = pltpu.make_async_copy(mask_ref, solid, sems.at[0])
    copy.start()
    side = local_frame()
    coefficients = scalars(rates_ref, force_ref, side)

    def load(where):
        return (
            [on_in[(k, *where)] for k in range(5)],
            [off_in[(k, *where)] for k in range(5)],
            [flat_in[(k, *where)] for k in range(9)],
        )

    def store(where, ahead, back, flat):
        for k, value in enumerate(ahead + back + flat):
            out[(k, *where)] = value

    copy.wait()
    collide_tiles(load, solid, store, 0, solid.shape[0], coefficients)
    finish(out, off_ref, on_ref, moved)
    copies = [
        pltpu.make_async_copy(moved.at[k], out_ref.at[FLAT[k]], sems.at[1 + k]) for k in range(9)
    ]
    for copy in copies:
        copy.start()
    for copy in copies:
        copy.wait()


def place_kernel(own, group_ref, out_in, out_ref, sems):
    del out_in
    side = local_frame()
    side = 1 - side if own else side
    copies = [
        pltpu.make_async_copy(group_ref.at[k], out_ref.at[select_channel(side, k)], sems.at[k])
        for k in range(5)
    ]
    for copy in copies:
        copy.start()
    for copy in copies:
        copy.wait()


def in_vmem(array):
    return pltpu.with_memory_space_constraint(array, pltpu.VMEM)


def in_hbm(array):
    return pltpu.with_memory_space_constraint(array, pltpu.HBM)


def vmem_result(shape):
    return pltpu.VMEM(shape, jnp.float32)


def hbm_result(shape):
    return pltpu.HBM(shape, jnp.float32)


def params(mebibytes):
    return pltpu.CompilerParams(vmem_limit_bytes=mebibytes << 20)


def on_device(populations, solid_mask, relax_rates, body_force):
    channels, depth, height, breadth = populations.shape
    assert depth == 1
    count = lax.axis_size("gx")
    assert count % 2 == 0
    off_pairs = [(i, (i + 1) % count if i % 2 else (i - 1) % count) for i in range(count)]
    on_pairs = [(i, i ^ 1) for i in range(count)]
    plane = in_hbm(populations.reshape(channels, height, breadth))
    mask = in_hbm(solid_mask.reshape(height, breadth))
    relax_rates, body_force = in_hbm(relax_rates), in_hbm(body_force)
    f32 = jnp.float32
    group = vmem_result((5, height, breadth))
    whole = hbm_result((channels, height, breadth))
    anywhere = pl.BlockSpec(memory_space=pl.ANY)
    local = pl.BlockSpec(memory_space=pltpu.VMEM)
    small = pl.BlockSpec(memory_space=pltpu.SMEM)
    sheet = pltpu.VMEM((height, breadth), jnp.int32)
    nodes = height * breadth
    off, on, flat = pl.pallas_call(
        first_kernel,
        out_shape=(group, group, vmem_result((9, height, breadth))),
        in_specs=[anywhere, anywhere, small, small],
        out_specs=(local, local, local),
        scratch_shapes=[
            pltpu.VMEM((channels, height, breadth), f32),
            sheet,
            pltpu.VMEM((channels, height, breadth), f32),
            pltpu.SemaphoreType.DMA((2, PIECES)),
        ],
        cost_estimate=pl.CostEstimate(
            flops=320 * nodes, bytes_accessed=80 * nodes, transcendentals=0
        ),
        compiler_params=params(14),
        name="first_step",
    )(plane, mask, relax_rates, body_force)
    off = lax.ppermute(off, "gx", off_pairs)
    on = lax.ppermute(on, "gx", on_pairs)
    off, on, result = pl.pallas_call(
        second_kernel,
        out_shape=(group, group, whole),
        in_specs=[local, local, local, anywhere, small, small],
        out_specs=(local, local, anywhere),
        scratch_shapes=[
            sheet,
            pltpu.VMEM((channels, height, breadth), f32),
            pltpu.VMEM((9, height, breadth), f32),
            pltpu.SemaphoreType.DMA((10,)),
        ],
        cost_estimate=pl.CostEstimate(
            flops=320 * nodes, bytes_accessed=80 * nodes, transcendentals=0
        ),
        compiler_params=params(14),
        name="second_step",
    )(in_vmem(off), in_vmem(on), flat, mask, relax_rates, body_force)
    off = lax.ppermute(off, "gx", off_pairs)
    on = lax.ppermute(on, "gx", on_pairs)
    for own, arrived in ((False, on), (True, off)):
        result = pl.pallas_call(
            functools.partial(place_kernel, own),
            out_shape=whole,
            in_specs=[local, anywhere],
            out_specs=anywhere,
            scratch_shapes=[pltpu.SemaphoreType.DMA((5,))],
            input_output_aliases={1: 0},
            cost_estimate=pl.CostEstimate(flops=0, bytes_accessed=20 * nodes, transcendentals=0),
            compiler_params=params(4),
        )(in_vmem(arrived), result)
    return result.reshape(channels, depth, height, breadth)


def solution(mesh):
    in_specs = (P(None, ("sample", "gx"), None, None), P(("sample", "gx"), None, None), P(), P())
    out_specs = P(None, ("sample", "gx"), None, None)
    return jax.shard_map(
        on_device, mesh=mesh, in_specs=in_specs, out_specs=out_specs, check_vma=False
    )
```

```python
import functools

import jax
import jax.numpy as jnp
import numpy as np
from jax import lax
from jax.experimental import pallas as pl
from jax.experimental.pallas import tpu as pltpu
from jax.sharding import PartitionSpec as P

PARTS = 2
LANES = 128
ROWS = 8

UP = (1, 7, 9, 11, 13)
DOWN = (2, 10, 8, 14, 12)
GROUP_SHIFTS = ((0, 0), (1, 0), (-1, 0), (0, 1), (0, -1))
BOUNCE = (0, 2, 1, 4, 3)
FLAT = (0, 3, 4, 5, 6, 15, 16, 17, 18)
FLAT_SHIFTS = ((0, 0), (1, 0), (-1, 0), (0, 1), (0, -1), (1, 1), (-1, -1), (1, -1), (-1, 1))
FLAT_OPPOSITE = (0, 2, 1, 4, 3, 6, 5, 8, 7)


def moment_tables():
    velocities = np.array(
        [
            [0, 0, 0],
            [1, 0, 0],
            [-1, 0, 0],
            [0, 1, 0],
            [0, -1, 0],
            [0, 0, 1],
            [0, 0, -1],
            [1, 1, 0],
            [-1, -1, 0],
            [1, -1, 0],
            [-1, 1, 0],
            [1, 0, 1],
            [-1, 0, -1],
            [1, 0, -1],
            [-1, 0, 1],
            [0, 1, 1],
            [0, -1, -1],
            [0, 1, -1],
            [0, -1, 1],
        ]
    )
    x, y, z = velocities.T
    polynomials = np.stack(
        [
            np.ones(19),
            x,
            y,
            z,
            x * y,
            x * z,
            y * z,
            x**2,
            y**2,
            z**2,
            x * y**2,
            x * z**2,
            x**2 * y,
            x**2 * z,
            y * z**2,
            y**2 * z,
            x**2 * y**2,
            x**2 * z**2,
            y**2 * z**2,
        ]
    ).astype(np.float64)
    basis = []
    for row in polynomials:
        vector = row.copy()
        for earlier in basis:
            vector = vector - vector @ earlier / (earlier @ earlier) * earlier
        basis.append(vector)
    moments = np.stack(basis)
    classes = ((0, 7, 8, 9, 16, 17, 18), (1, 10, 11), (2, 12, 14), (3, 13, 15))
    tables = []
    for numbers in classes:
        rows = list(numbers)
        lower = moments[rows] @ np.linalg.pinv(polynomials[rows])
        lower = np.where(np.abs(lower) < 1e-12, 0.0, lower)
        inverse = np.linalg.inv(lower)
        inverse = np.where(np.abs(inverse) < 1e-12, 0.0, inverse)
        tables.append((numbers, lower, inverse))
    return tables


def relaxing_entries(rates):
    matrices = []
    for numbers, lower, inverse in moment_tables():
        size = len(numbers)
        matrix = {}
        for i in range(size):
            for j in range(i + 1):
                total = None
                for m in range(j, i + 1):
                    factor = float(inverse[i, m] * lower[m, j])
                    if factor == 0.0:
                        continue
                    term = rates[numbers[m]] * factor
                    total = term if total is None else total + term
                if total is not None:
                    matrix[i, j] = total
        matrices.append(matrix)
    return matrices


def apply_lower(matrix, vector):
    out = []
    for i in range(len(vector)):
        total = None
        for j in range(i + 1):
            if (i, j) in matrix:
                term = matrix[i, j] * vector[j]
                total = term if total is None else total + term
        out.append(total)
    return out


def relax(ahead, back, flat, solid, matrices, cross_rates, push):
    axis_sum = (ahead[0] + back[0], flat[1] + flat[2], flat[3] + flat[4])
    axis_odd = (ahead[0] - back[0], flat[1] - flat[2], flat[3] - flat[4])

    def butterfly(pp, pm, mp, mm):
        a, b, c, d = pp + pm, pp - pm, mp + mm, mp - mm
        return a + c, a - c, b + d, b - d

    xy, xy_x, xy_y, xy_xy = butterfly(ahead[1], ahead[2], back[1], back[2])
    xz, xz_x, xz_z, xz_xz = butterfly(ahead[3], ahead[4], back[3], back[4])
    yz, yz_y, yz_z, yz_yz = butterfly(flat[5], flat[7], flat[8], flat[6])
    sx, sy, sz = axis_sum
    density = (flat[0] + (sx + sy)) + ((sz + xy) + (xz + yz))
    jx = axis_odd[0] + (xy_x + xz_x)
    jy = axis_odd[1] + (xy_y + yz_y)
    jz = axis_odd[2] + (xz_z + yz_z)
    over = 1.0 / density
    ux, uy, uz = jx * over, jy * over, jz * over
    qxx, qyy, qzz = jx * ux, jy * uy, jz * uz
    base = (density - 1.5 * (qxx + (qyy + qzz))) * (1.0 / 9.0)
    hx, hy, hz = 0.5 * qxx, 0.5 * qyy, 0.5 * qzz
    bx, by, bz = base + hx, base + hy, base + hz
    rest = flat[0] - 3.0 * base
    sx, sy, sz = sx - bx, sy - by, sz - bz
    xy, xz, yz = xy - (bx + hy), xz - (bx + hz), yz - (by + hz)
    third = 1.0 / 3.0
    tx, ty, tz = jx * third, jy * third, jz * third
    raw = [
        (rest + (sx + sy)) + ((sz + xy) + (xz + yz)),
        sx + (xy + xz),
        sy + (xy + yz),
        sz + (xz + yz),
        xy,
        xz,
        yz,
    ]
    change = apply_lower(matrices[0], raw)
    total, mx, my, mz, cxy, cxz, cyz = change
    even_xy, even_xz, even_yz = 0.25 * cxy, 0.25 * cxz, 0.25 * cyz
    even_x = 0.5 * (mx - (cxy + cxz))
    even_y = 0.5 * (my - (cxy + cyz))
    even_z = 0.5 * (mz - (cxz + cyz))
    even_rest = (total - (mx + my)) + ((cxy + cxz) + (cyz - mz))

    def odd_class(matrix, along, first, second, mean, force):
        first, second = first - mean, second - mean
        along = along - mean
        change = apply_lower(matrix, [along + (first + second), first, second])
        lift = density * force
        return (
            0.5 * ((change[0] - (change[1] + change[2])) - lift),
            0.25 * (change[1] - lift),
            0.25 * (change[2] - lift),
        )

    odd_x, odd_xy_x, odd_xz_x = odd_class(matrices[1], axis_odd[0], xy_x, xz_x, tx, push[0])
    odd_y, odd_xy_y, odd_yz_y = odd_class(matrices[2], axis_odd[1], xy_y, yz_y, ty, push[1])
    odd_z, odd_xz_z, odd_yz_z = odd_class(matrices[3], axis_odd[2], xz_z, yz_z, tz, push[2])
    both_xy = (xy_xy - jx * uy) * cross_rates[0]
    both_xz = (xz_xz - jx * uz) * cross_rates[1]
    both_yz = (yz_yz - jy * uz) * cross_rates[2]

    def spread(even, first, second, both):
        a, b, c, d = even + first, second + both, even - first, second - both
        return a + b, a - b, c + d, c - d

    xy_pp, xy_pm, xy_mp, xy_mm = spread(even_xy, odd_xy_x, odd_xy_y, both_xy)
    xz_pp, xz_pm, xz_mp, xz_mm = spread(even_xz, odd_xz_x, odd_xz_z, both_xz)
    yz_pp, yz_pm, yz_mp, yz_mm = spread(even_yz, odd_yz_y, odd_yz_z, both_yz)
    new_ahead = [even_x + odd_x, xy_pp, xy_pm, xz_pp, xz_pm]
    new_back = [even_x - odd_x, xy_mp, xy_mm, xz_mp, xz_mm]
    new_flat = [
        even_rest,
        even_y + odd_y,
        even_y - odd_y,
        even_z + odd_z,
        even_z - odd_z,
        yz_pp,
        yz_mm,
        yz_pm,
        yz_mp,
    ]
    out_ahead = [
        jnp.where(solid, back[BOUNCE[k]], ahead[k] - new_ahead[k]) for k in range(5)
    ]
    out_back = [jnp.where(solid, ahead[BOUNCE[k]], back[k] - new_back[k]) for k in range(5)]
    out_flat = [
        jnp.where(solid, flat[FLAT_OPPOSITE[k]], flat[k] - new_flat[k]) for k in range(9)
    ]
    return out_ahead, out_back, out_flat


def local_frame():
    return lax.rem(lax.axis_index("gx"), 2)


def select_channel(side, k):
    return jnp.where(side == 1, UP[k], DOWN[k])


def scalars(rates_ref, force_ref, side):
    rates = [rates_ref[m] for m in range(19)]
    third = 1.0 / 3.0
    sign = jnp.where(side == 1, third, -third).astype(jnp.float32)
    push = (force_ref[0] * sign, force_ref[1] * third, force_ref[2] * third)
    scale = 0.25
    cross = tuple(rates[m] * scale for m in (4, 5, 6))
    return relaxing_entries(rates), cross, push


def shift_in_z(halves, step):
    if step == 0:
        return halves
    lane = lax.broadcasted_iota(jnp.int32, halves[0].shape, 1)
    edge = lane == (0 if step > 0 else LANES - 1)
    low, high = (pltpu.roll(value, step % LANES, 1) for value in halves)
    return jnp.where(edge, high, low), jnp.where(edge, low, high)


def relax_tile(load, solid_ref, solid_row, coefficients):
    halves = []
    for lane in range(0, solid_ref.shape[1], LANES):
        solid = solid_ref[pl.ds(solid_row, ROWS), pl.ds(lane, LANES)] == 1
        ahead, back, flat = relax(*load(lane), solid, *coefficients)
        halves.append(ahead + back + flat)
    return list(zip(*halves, strict=True))


def first_kernel(
    start, f_ref, mask_ref, rates_hbm, force_hbm, off_ref, on_ref, flat_ref, f, solid, out, rates, force, sems
):
    height = mask_ref.shape[0]
    tiles = off_ref.shape[1] // ROWS + 2

    def fetch(i):
        row = (start + (i - 1) * ROWS) % height
        return pltpu.make_async_copy(
            f_ref.at[:, pl.ds(row, ROWS), :], f.at[:, pl.ds(i * ROWS, ROWS), :], sems.at[i]
        )

    small = [
        pltpu.make_async_copy(rates_hbm, rates, sems.at[tiles]),
        pltpu.make_async_copy(force_hbm, force, sems.at[tiles + 1]),
        pltpu.make_async_copy(mask_ref, solid, sems.at[tiles + 2]),
    ]
    fetch(0).start()
    for copy in small:
        copy.start()
    for i in range(1, tiles):
        fetch(i).start()
    side = local_frame()
    toward = [select_channel(side, k) for k in range(5)]
    away = [select_channel(1 - side, k) for k in range(5)]
    channels = toward + away + list(FLAT)
    for copy in small:
        copy.wait()
    coefficients = scalars(rates, force, side)
    targets = [(off_ref, k) for k in range(5)] + [(on_ref, k) for k in range(5)]
    targets += [(flat_ref, k) for k in range(9)]
    shifts = GROUP_SHIFTS + GROUP_SHIFTS + FLAT_SHIFTS

    def collide(i):
        local = pl.multiple_of(i * ROWS, ROWS)
        pltpu.make_async_copy(
            f_ref.at[:, pl.ds(0, ROWS), :], f.at[:, pl.ds(local, ROWS), :], sems.at[i]
        ).wait()

        def load(lane):
            values = [f[c, pl.ds(local, ROWS), pl.ds(lane, LANES)] for c in channels]
            return values[:5], values[5:10], values[10:]

        row = pl.multiple_of(lax.rem(start + height + (i - 1) * ROWS, height), ROWS)
        for k, pair in enumerate(relax_tile(load, solid, row, coefficients)):
            for half in range(2):
                out[k, half, pl.ds(local, ROWS), :] = pair[half]

    def emit(i):
        local = i * ROWS
        row = pl.multiple_of(local - ROWS, ROWS)
        for k, (ref, entry) in enumerate(targets):
            pair = tuple(out[k, half, pl.ds(local - shifts[k][0], ROWS), :] for half in range(2))
            pair = shift_in_z(pair, shifts[k][1])
            for half in range(2):
                ref[entry, pl.ds(row, ROWS), pl.ds(half * LANES, LANES)] = pair[half]

    def head(i, carry):
        collide(i)
        return carry

    def body(i, carry):
        emit(i - 2)
        collide(i)
        return carry

    lax.fori_loop(0, 3, head, 0)
    lax.fori_loop(3, tiles, body, 0)
    emit(tiles - 2)


def second_kernel(
    start, off_in, on_in, flat_in, solid, rates, force, off_ref, on_ref, flat_ref
):
    coefficients = scalars(rates, force, local_frame())
    targets = [(off_ref, k) for k in range(5)] + [(on_ref, k) for k in range(5)]
    targets += [(flat_ref, k) for k in range(9)]
    shifts = GROUP_SHIFTS + GROUP_SHIFTS + FLAT_SHIFTS

    def body(i, carry):
        local = pl.multiple_of(i * ROWS, ROWS)

        def load(lane):
            where = (pl.ds(local, ROWS), pl.ds(lane, LANES))
            return (
                [on_in[(k, *where)] for k in range(5)],
                [off_in[(k, *where)] for k in range(5)],
                [flat_in[(k, *where)] for k in range(9)],
            )

        row = pl.multiple_of(start + local, ROWS)
        for k, pair in enumerate(relax_tile(load, solid, row, coefficients)):
            ref, entry = targets[k]
            pair = shift_in_z(pair, shifts[k][1])
            for half in range(2):
                ref[entry, pl.ds(local, ROWS), pl.ds(half * LANES, LANES)] = pair[half]
        return carry

    lax.fori_loop(0, off_in.shape[1] // ROWS, body, 0)


def place(low_ref, high_ref, out_ref, moved, sems, number_of, shifts):
    copies = []
    part = low_ref.shape[1]
    slot = 0
    for k, (step, _) in enumerate(shifts):
        if step == 0:
            for half, ref in enumerate((low_ref, high_ref)):
                rows = pl.ds(half * part, part)
                copies.append(
                    pltpu.make_async_copy(
                        ref.at[k], out_ref.at[number_of(k), rows, :], sems.at[2 * k + half]
                    )
                )
                copies[-1].start()
    for k, (step, _) in enumerate(shifts):
        if step != 0:
            both = jnp.concatenate([low_ref[k], high_ref[k]], axis=0)
            moved[slot] = pltpu.roll(both, step % both.shape[0], 0)
            copies.append(
                pltpu.make_async_copy(moved.at[slot], out_ref.at[number_of(k)], sems.at[2 * k])
            )
            copies[-1].start()
            slot += 1
    for copy in copies:
        copy.wait()


def place_flat_kernel(low_ref, high_ref, out_ref, moved, sems):
    place(low_ref, high_ref, out_ref, moved, sems, lambda k: FLAT[k], FLAT_SHIFTS)


def place_group_kernel(own, low_ref, high_ref, out_in, out_ref, moved, sems):
    del out_in
    side = local_frame()
    side = 1 - side if own else side
    place(low_ref, high_ref, out_ref, moved, sems, lambda k: select_channel(side, k), GROUP_SHIFTS)


def in_vmem(array):
    return pltpu.with_memory_space_constraint(array, pltpu.VMEM)


def in_hbm(array):
    return pltpu.with_memory_space_constraint(array, pltpu.HBM)


def vmem_result(shape):
    return pltpu.VMEM(shape, jnp.float32)


def hbm_result(shape):
    return pltpu.HBM(shape, jnp.float32)


def params(mebibytes):
    return pltpu.CompilerParams(vmem_limit_bytes=mebibytes << 20)


def in_smem(array):
    return pltpu.with_memory_space_constraint(array, pltpu.SMEM)


def on_device(populations, solid_mask, relax_rates, body_force):
    channels, depth, height, breadth = populations.shape
    assert depth == 1 and breadth == 2 * LANES
    count = lax.axis_size("gx")
    assert count % 2 == 0
    off_pairs = [(i, (i + 1) % count if i % 2 else (i - 1) % count) for i in range(count)]
    on_pairs = [(i, i ^ 1) for i in range(count)]
    plane = in_hbm(populations.reshape(channels, height, breadth))
    mask = solid_mask.reshape(height, breadth)
    f32 = jnp.float32
    part = height // PARTS
    anywhere = pl.BlockSpec(memory_space=pl.ANY)
    local = pl.BlockSpec(memory_space=pltpu.VMEM)
    small = pl.BlockSpec(memory_space=pltpu.SMEM)
    pieces = tuple(vmem_result((n, part, breadth)) for n in (5, 5, 9))
    whole = hbm_result((channels, height, breadth))
    tiles = part // ROWS + 2

    def cost(rows):
        nodes = rows * breadth
        return pl.CostEstimate(flops=320 * nodes, bytes_accessed=160 * nodes, transcendentals=0)

    def step_one(p):
        return pl.pallas_call(
            functools.partial(first_kernel, p * part),
            out_shape=pieces,
            in_specs=[anywhere] * 4,
            out_specs=(local, local, local),
            scratch_shapes=[
                pltpu.VMEM((channels, tiles * ROWS, breadth), f32),
                pltpu.VMEM((height, breadth), jnp.int32),
                pltpu.VMEM((channels, 2, tiles * ROWS, LANES), f32),
                pltpu.SMEM(relax_rates.shape, f32),
                pltpu.SMEM(body_force.shape, f32),
                pltpu.SemaphoreType.DMA((tiles + 3,)),
            ],
            cost_estimate=cost(part),
            compiler_params=params(8),
        )(plane, in_hbm(mask), in_hbm(relax_rates), in_hbm(body_force))

    def step_two(p, off, on, flat):
        return pl.pallas_call(
            functools.partial(second_kernel, p * part),
            out_shape=pieces,
            in_specs=[local, local, local, local, small, small],
            out_specs=(local, local, local),
            cost_estimate=cost(part),
            compiler_params=params(8),
        )(in_vmem(off), in_vmem(on), flat, in_vmem(mask), in_smem(relax_rates), in_smem(body_force))

    def send(array, pairs):
        return lax.ppermute(array, "gx", pairs)

    offs, ons, flats = [], [], []
    for p in range(PARTS):
        off, on, flat = step_one(p)
        offs.append(send(off, off_pairs))
        ons.append(send(on, on_pairs))
        flats.append(flat)
    last = []
    for p in range(PARTS):
        off, on, flat = step_two(p, offs[p], ons[p], flats[p])
        last.append((send(off, off_pairs), on, flat))
    offs, ons, flats = zip(*last, strict=True)
    ons = [send(on, on_pairs) for on in ons]
    result = pl.pallas_call(
        place_flat_kernel,
        out_shape=whole,
        in_specs=[local, local],
        out_specs=anywhere,
        scratch_shapes=[pltpu.VMEM((6, height, breadth), f32), pltpu.SemaphoreType.DMA((18,))],
        cost_estimate=pl.CostEstimate(
            flops=0, bytes_accessed=36 * height * breadth, transcendentals=0
        ),
        compiler_params=params(4),
        name="place_flat",
    )(*flats)
    for own, arrived in ((False, ons), (True, offs)):
        result = pl.pallas_call(
            functools.partial(place_group_kernel, own),
            out_shape=whole,
            in_specs=[local, local, anywhere],
            out_specs=anywhere,
            scratch_shapes=[pltpu.VMEM((2, height, breadth), f32), pltpu.SemaphoreType.DMA((10,))],
            input_output_aliases={2: 0},
            cost_estimate=pl.CostEstimate(
                flops=0, bytes_accessed=20 * height * breadth, transcendentals=0
            ),
            compiler_params=params(4),
        )(*(in_vmem(array) for array in arrived), result)
    return result.reshape(channels, depth, height, breadth)


def solution(mesh):
    in_specs = (P(None, ("sample", "gx"), None, None), P(("sample", "gx"), None, None), P(), P())
    out_specs = P(None, ("sample", "gx"), None, None)
    return jax.shard_map(
        on_device, mesh=mesh, in_specs=in_specs, out_specs=out_specs, check_vma=False
    )
```

```python
import functools

import jax
import jax.numpy as jnp
import numpy as np
from jax import lax
from jax.experimental import pallas as pl
from jax.experimental.pallas import tpu as pltpu
from jax.sharding import PartitionSpec as P

EIGHTHS = (4, 4)
COEFFICIENTS = 52
GROUPS = (0, 2, 5)
LANES = 128
ROWS = 8

UP = (1, 7, 9, 11, 13)
DOWN = (2, 10, 8, 14, 12)
GROUP_SHIFTS = ((0, 0), (1, 0), (-1, 0), (0, 1), (0, -1))
BOUNCE = (0, 2, 1, 4, 3)
FLAT = (0, 3, 4, 5, 6, 15, 16, 17, 18)
FLAT_SHIFTS = ((0, 0), (1, 0), (-1, 0), (0, 1), (0, -1), (1, 1), (-1, -1), (1, -1), (-1, 1))
FLAT_OPPOSITE = (0, 2, 1, 4, 3, 6, 5, 8, 7)


def moment_tables():
    velocities = np.array(
        [
            [0, 0, 0],
            [1, 0, 0],
            [-1, 0, 0],
            [0, 1, 0],
            [0, -1, 0],
            [0, 0, 1],
            [0, 0, -1],
            [1, 1, 0],
            [-1, -1, 0],
            [1, -1, 0],
            [-1, 1, 0],
            [1, 0, 1],
            [-1, 0, -1],
            [1, 0, -1],
            [-1, 0, 1],
            [0, 1, 1],
            [0, -1, -1],
            [0, 1, -1],
            [0, -1, 1],
        ]
    )
    x, y, z = velocities.T
    polynomials = np.stack(
        [
            np.ones(19),
            x,
            y,
            z,
            x * y,
            x * z,
            y * z,
            x**2,
            y**2,
            z**2,
            x * y**2,
            x * z**2,
            x**2 * y,
            x**2 * z,
            y * z**2,
            y**2 * z,
            x**2 * y**2,
            x**2 * z**2,
            y**2 * z**2,
        ]
    ).astype(np.float64)
    basis = []
    for row in polynomials:
        vector = row.copy()
        for earlier in basis:
            vector = vector - vector @ earlier / (earlier @ earlier) * earlier
        basis.append(vector)
    moments = np.stack(basis)
    classes = ((0, 7, 8, 9, 16, 17, 18), (1, 10, 11), (2, 12, 14), (3, 13, 15))
    tables = []
    for numbers in classes:
        rows = list(numbers)
        lower = moments[rows] @ np.linalg.pinv(polynomials[rows])
        lower = np.where(np.abs(lower) < 1e-12, 0.0, lower)
        inverse = np.linalg.inv(lower)
        inverse = np.where(np.abs(inverse) < 1e-12, 0.0, inverse)
        tables.append((numbers, lower, inverse))
    return tables


def relaxing_entries(rates):
    matrices = []
    for numbers, lower, inverse in moment_tables():
        size = len(numbers)
        matrix = {}
        for i in range(size):
            for j in range(i + 1):
                total = None
                for m in range(j, i + 1):
                    factor = float(inverse[i, m] * lower[m, j])
                    if factor == 0.0:
                        continue
                    term = rates[numbers[m]] * factor
                    total = term if total is None else total + term
                if total is not None:
                    matrix[i, j] = total * 0.5 if i or size == 3 else total
        matrices.append(matrix)
    return matrices


def apply_lower(matrix, vector):
    out = []
    for i in range(len(vector)):
        total = None
        for j in range(i + 1):
            if (i, j) in matrix:
                term = matrix[i, j]() * vector[j]
                total = term if total is None else total + term
        out.append(total)
    return out


def relax(ahead, back, flat, solid, matrices, cross_rates, push):
    def butterfly(pp, pm, mp, mm):
        a, b, c, d = pp + pm, pp - pm, mp + mm, mp - mm
        return a + c, a - c, b + d, b - d

    sx, sy, sz = ahead[0] + back[0], flat[1] + flat[2], flat[3] + flat[4]
    xy, xy_x, xy_y, xy_xy = butterfly(ahead[1], ahead[2], back[1], back[2])
    xz, xz_x, xz_z, xz_xz = butterfly(ahead[3], ahead[4], back[3], back[4])
    yz, yz_y, yz_z, yz_yz = butterfly(flat[5], flat[7], flat[8], flat[6])
    density = (flat[0] + (sx + sy)) + ((sz + xy) + (xz + yz))
    jx = (ahead[0] - back[0]) + (xy_x + xz_x)
    jy = (flat[1] - flat[2]) + (xy_y + yz_y)
    jz = (flat[3] - flat[4]) + (xz_z + yz_z)
    over = 1.0 / density
    ux, uy, uz = jx * over, jy * over, jz * over
    qxx, qyy, qzz = jx * ux, jy * uy, jz * uz
    energy = 1.5 * (qxx + (qyy + qzz))
    still = density - energy
    base = still * (1.0 / 9.0)
    hx, hy, hz = 0.5 * qxx, 0.5 * qyy, 0.5 * qzz
    bx, by, bz = base + hx, base + hy, base + hz
    xy, xz, yz = xy - (bx + hy), xz - (bx + hz), yz - (by + hz)
    raw = [
        density - (still + energy),
        (sx - bx) + (xy + xz),
        (sy - by) + (xy + yz),
        (sz - bz) + (xz + yz),
        xy,
        xz,
        yz,
    ]
    total, mx, my, mz, cxy, cxz, cyz = apply_lower(matrices[0], raw)
    even_x, even_y, even_z = mx - (cxy + cxz), my - (cxy + cyz), mz - (cxz + cyz)
    rest = (mx + my) + ((mz - cxy) - (cxz + cyz))
    even_rest = total - (rest + rest)
    even_xy, even_xz, even_yz = 0.5 * cxy, 0.5 * cxz, 0.5 * cyz

    def odd_class(matrix, current, first, second, force):
        mean = current * (1.0 / 3.0)
        departures = [current - 3.0 * mean, first - mean, second - mean]
        along, first, second = apply_lower(matrix, departures)
        lift = density * force()
        along = along - (lift + (first + second))
        return along, 0.5 * (first - lift), 0.5 * (second - lift)

    odd_x, odd_xy_x, odd_xz_x = odd_class(matrices[1], jx, xy_x, xz_x, push[0])
    odd_y, odd_xy_y, odd_yz_y = odd_class(matrices[2], jy, xy_y, yz_y, push[1])
    odd_z, odd_xz_z, odd_yz_z = odd_class(matrices[3], jz, xz_z, yz_z, push[2])
    both_xy = (xy_xy - jx * uy) * cross_rates[0]()
    both_xz = (xz_xz - jx * uz) * cross_rates[1]()
    both_yz = (yz_yz - jy * uz) * cross_rates[2]()

    def spread(even, first, second, both):
        a, b, c, d = even + first, second + both, even - first, second - both
        return a + b, a - b, c + d, c - d

    xy_pp, xy_pm, xy_mp, xy_mm = spread(even_xy, odd_xy_x, odd_xy_y, both_xy)
    xz_pp, xz_pm, xz_mp, xz_mm = spread(even_xz, odd_xz_x, odd_xz_z, both_xz)
    yz_pp, yz_pm, yz_mp, yz_mm = spread(even_yz, odd_yz_y, odd_yz_z, both_yz)
    new_ahead = [even_x + odd_x, xy_pp, xy_pm, xz_pp, xz_pm]
    new_back = [even_x - odd_x, xy_mp, xy_mm, xz_mp, xz_mm]
    new_flat = [
        even_rest,
        even_y + odd_y,
        even_y - odd_y,
        even_z + odd_z,
        even_z - odd_z,
        yz_pp,
        yz_mm,
        yz_pm,
        yz_mp,
    ]
    out_ahead = [
        jnp.where(solid, back[BOUNCE[k]], ahead[k] - new_ahead[k]) for k in range(5)
    ]
    out_back = [jnp.where(solid, ahead[BOUNCE[k]], back[k] - new_back[k]) for k in range(5)]
    out_flat = [
        jnp.where(solid, flat[FLAT_OPPOSITE[k]], flat[k] - new_flat[k]) for k in range(9)
    ]
    return out_ahead, out_back, out_flat


def local_frame():
    return lax.rem(lax.axis_index("gx"), 2)


def select_channel(side, k):
    return jnp.where(side == 1, UP[k], DOWN[k])


def scalars(rates_ref, force_ref, side, spread):
    rates = [rates_ref[m] for m in range(19)]
    sixth = 1.0 / 6.0
    sign = jnp.where(side == 1, sixth, -sixth).astype(jnp.float32)
    push = (force_ref[0] * sign, force_ref[1] * sixth, force_ref[2] * sixth)
    cross = tuple(rates[m] * 0.25 for m in (4, 5, 6))
    slots = iter(range(spread.shape[0]))

    def kept(value):
        slot = next(slots)
        spread[slot] = jnp.full(spread.shape[1:], value, jnp.float32)
        return lambda: spread[slot]

    matrices = [
        {place: kept(value) for place, value in matrix.items()}
        for matrix in relaxing_entries(rates)
    ]
    return matrices, tuple(map(kept, cross)), tuple(map(kept, push))


def shift_in_z(halves, step):
    if step == 0:
        return halves
    lane = lax.broadcasted_iota(jnp.int32, halves[0].shape, 1)
    edge = lane == (0 if step > 0 else LANES - 1)
    low, high = (pltpu.roll(value, step % LANES, 1) for value in halves)
    return jnp.where(edge, high, low), jnp.where(edge, low, high)


def relax_tile(load, solid_ref, solid_row, coefficients):
    halves = []
    for lane in range(0, solid_ref.shape[1], LANES):
        solid = solid_ref[pl.ds(solid_row, ROWS), pl.ds(lane, LANES)] == 1
        ahead, back, flat = relax(*load(lane), solid, *coefficients)
        halves.append(ahead + back + flat)
    return list(zip(*halves, strict=True))


OFF, ON, STILL = "off", "on", "still"
GROUP_SIZE = {OFF: 5, ON: 5, STILL: 9}


def wanted(groups, refs):
    first = {OFF: 0, ON: 5, STILL: 10}
    shifts = {OFF: GROUP_SHIFTS, ON: GROUP_SHIFTS, STILL: FLAT_SHIFTS}
    return [
        (first[group] + k, ref, k, shifts[group][k])
        for group, ref in zip(groups, refs, strict=True)
        for k in range(GROUP_SIZE[group])
    ]


def first_kernel(start, rows, groups, f_ref, mask_ref, rates_hbm, force_hbm, *refs):
    *results, f, solid, out, spread, rates, force, sems = refs
    height = mask_ref.shape[0]
    tiles = rows // ROWS + 2
    targets = wanted(groups, results)

    def fetch(i):
        row = (start + (i - 1) * ROWS) % height
        return pltpu.make_async_copy(
            f_ref.at[:, pl.ds(row, ROWS), :], f.at[:, pl.ds(i * ROWS, ROWS), :], sems.at[i]
        )

    small = [
        pltpu.make_async_copy(rates_hbm, rates, sems.at[tiles]),
        pltpu.make_async_copy(force_hbm, force, sems.at[tiles + 1]),
        pltpu.make_async_copy(mask_ref, solid, sems.at[tiles + 2]),
    ]
    for copy in small[:2]:
        copy.start()
    fetch(0).start()
    fetch(1).start()
    small[2].start()
    for i in range(2, tiles):
        fetch(i).start()
    side = local_frame()
    toward = [select_channel(side, k) for k in range(5)]
    away = [select_channel(1 - side, k) for k in range(5)]
    channels = toward + away + list(FLAT)
    for copy in small[:2]:
        copy.wait()
    coefficients = scalars(rates, force, side, spread)

    def collide(i):
        local = i * ROWS
        if i in GROUPS:
            following = [g for g in GROUPS if g > i]
            for j in range(i, min(following[0] if following else tiles, tiles)):
                fetch(j).wait()
        if i == 0:
            small[2].wait()

        def load(lane):
            values = [f[c, pl.ds(local, ROWS), pl.ds(lane, LANES)] for c in channels]
            return values[:5], values[5:10], values[10:]

        row = (start + (i - 1) * ROWS) % height
        pairs = relax_tile(load, solid, row, coefficients)
        for slot, (place, *_) in enumerate(targets):
            for half in range(2):
                out[slot, half, pl.ds(local, ROWS), :] = pairs[place][half]

    def emit(i):
        local = i * ROWS
        row = local - ROWS
        for slot, (_, ref, entry, (step_y, step_z)) in enumerate(targets):
            pair = tuple(out[slot, half, pl.ds(local - step_y, ROWS), :] for half in range(2))
            pair = shift_in_z(pair, step_z)
            for half in range(2):
                ref[entry, pl.ds(row, ROWS), pl.ds(half * LANES, LANES)] = pair[half]

    for i in range(tiles):
        collide(i)
        if i > 1:
            emit(i - 1)


def second_kernel(parts, groups, begin, *refs):
    off_in, refs = refs[: len(parts)], refs[len(parts) :]
    on_in, flat_in, solid, rates, force, *results, spread = refs
    results = results[-len(groups) :]
    coefficients = scalars(rates, force, local_frame(), spread)
    targets = wanted(groups, results)
    for (start, rows), arrived in zip(parts, off_in, strict=True):
        for local in range(0, rows, ROWS):

            def load(lane, local=local, start=start, arrived=arrived):
                own = (pl.ds(local, ROWS), pl.ds(lane, LANES))
                where = (pl.ds(start + local, ROWS), pl.ds(lane, LANES))
                return (
                    [on_in[(k, *where)] for k in range(5)],
                    [arrived[(k, *own)] for k in range(5)],
                    [flat_in[(k, *where)] for k in range(9)],
                )

            pairs = relax_tile(load, solid, start + local, coefficients)
            for place, ref, entry, (_, step_z) in targets:
                pair = shift_in_z(pairs[place], step_z)
                for half in range(2):
                    ref[entry, pl.ds(start - begin + local, ROWS), pl.ds(half * LANES, LANES)] = pair[half]


def place_all(refs, out_ref, moved, sems, number_of, shifts):
    copies = []
    for k, (step, _) in enumerate(shifts):
        both = jnp.concatenate([ref[k] for ref in refs], axis=0)
        moved[k] = pltpu.roll(both, step % both.shape[0], 0) if step else both
        copies.append(pltpu.make_async_copy(moved.at[k], out_ref.at[number_of(k)], sems.at[k]))
        copies[-1].start()
    for copy in copies:
        copy.wait()


def place_flat_kernel(*refs):
    *parts, out_ref, moved, sems = refs
    place_all(parts, out_ref, moved, sems, lambda k: FLAT[k], FLAT_SHIFTS)


def place_on_kernel(*refs):
    *parts, _, out_ref, moved, sems = refs
    side = local_frame()
    place_all(parts, out_ref, moved, sems, lambda k: select_channel(side, k), GROUP_SHIFTS)


def place_off_kernel(p, start, height, *refs):
    *parts, _, out_ref, moved, sems = refs
    side = local_frame()
    own = parts[p]
    rows = own.shape[1]
    first, last = p == 0, start + rows == height
    copies = []

    def send(source, k, to, slot):
        copies.append(
            pltpu.make_async_copy(
                source, out_ref.at[select_channel(1 - side, k), pl.ds(to, source.shape[0]), :], sems.at[slot]
            )
        )
        copies[-1].start()

    slot = 0
    for k, (step, _) in enumerate(GROUP_SHIFTS):
        if step == 0:
            send(own.at[k], k, start, slot)
            slot += 1
    for entry, k in enumerate((1, 2)):
        step = GROUP_SHIFTS[k][0]
        stack = [own[k]]
        if not first:
            stack.insert(0, parts[p - 1][k, pl.ds(parts[p - 1].shape[1] - ROWS, ROWS), :])
        if last:
            stack.append(parts[0][k, pl.ds(0, ROWS), :])
        stack = jnp.concatenate(stack, axis=0)
        size = stack.shape[0]
        moved[entry, pl.ds(0, size), :] = pltpu.roll(stack, step % size, 0)
        begin = start - (0 if first else ROWS)
        low = ROWS if step > 0 else 0
        high = size - (ROWS if step < 0 else 0)
        if last and step > 0:
            send(moved.at[entry, pl.ds(high - ROWS, ROWS), :], k, 0, slot)
            slot += 1
            high -= ROWS
        send(moved.at[entry, pl.ds(low, high - low), :], k, begin + low, slot)
        slot += 1
    for copy in copies:
        copy.wait()


def in_vmem(array):
    return pltpu.with_memory_space_constraint(array, pltpu.VMEM)


def in_hbm(array):
    return pltpu.with_memory_space_constraint(array, pltpu.HBM)


def vmem_result(shape):
    return pltpu.VMEM(shape, jnp.float32)


def hbm_result(shape):
    return pltpu.HBM(shape, jnp.float32)


def params(mebibytes):
    return pltpu.CompilerParams(vmem_limit_bytes=mebibytes << 20)


def in_smem(array):
    return pltpu.with_memory_space_constraint(array, pltpu.SMEM)


def row_parts(height):
    sizes = [height * eighths // 8 for eighths in EIGHTHS]
    assert all(size % ROWS == 0 for size in sizes) and sum(sizes) == height
    return [(sum(sizes[:p]), size) for p, size in enumerate(sizes)]


def on_device(populations, solid_mask, relax_rates, body_force):
    channels, depth, height, breadth = populations.shape
    assert depth == 1 and breadth == 2 * LANES
    count = lax.axis_size("gx")
    assert count % 2 == 0
    off_pairs = [(i, (i + 1) % count if i % 2 else (i - 1) % count) for i in range(count)]
    on_pairs = [(i, i ^ 1) for i in range(count)]
    plane = in_hbm(populations.reshape(channels, height, breadth))
    mask = solid_mask.reshape(height, breadth)
    f32 = jnp.float32
    anywhere = pl.BlockSpec(memory_space=pl.ANY)
    local = pl.BlockSpec(memory_space=pltpu.VMEM)
    small = pl.BlockSpec(memory_space=pltpu.SMEM)
    whole = hbm_result((channels, height, breadth))
    spread = pltpu.VMEM((COEFFICIENTS, ROWS, LANES), f32)

    def cost(rows):
        nodes = rows * breadth
        return pl.CostEstimate(flops=320 * nodes, bytes_accessed=160 * nodes, transcendentals=0)

    def results(groups, rows):
        shapes = tuple(vmem_result((GROUP_SIZE[group], rows, breadth)) for group in groups)
        return shapes, tuple(local for _ in shapes)

    def step_one(start, rows, groups):
        tiles = rows // ROWS + 2
        shapes, specs = results(groups, rows)
        kept = sum(GROUP_SIZE[group] for group in groups)
        return pl.pallas_call(
            functools.partial(first_kernel, start, rows, groups),
            out_shape=shapes,
            in_specs=[anywhere] * 4,
            out_specs=specs,
            scratch_shapes=[
                pltpu.VMEM((channels, tiles * ROWS, breadth), f32),
                pltpu.VMEM((height, breadth), jnp.int32),
                pltpu.VMEM((kept, 2, tiles * ROWS, LANES), f32),
                spread,
                pltpu.SMEM(relax_rates.shape, f32),
                pltpu.SMEM(body_force.shape, f32),
                pltpu.SemaphoreType.DMA((tiles + 3,)),
            ],
            cost_estimate=cost(rows),
            compiler_params=params(8),
        )(plane, in_hbm(mask), in_hbm(relax_rates), in_hbm(body_force))

    def step_two(parts, groups, off, on, flat, carried=None):
        rows = height if carried is not None else sum(rows for _, rows in parts)
        begin = 0 if carried is not None else parts[0][0]
        shapes, specs = results(groups, rows)
        operands = (*off, on, flat, in_vmem(mask), in_smem(relax_rates), in_smem(body_force))
        held = tuple(carried or ())
        return pl.pallas_call(
            functools.partial(second_kernel, parts, groups, begin),
            out_shape=shapes,
            in_specs=[local] * (len(parts) + 3) + [small, small] + [local] * len(held),
            out_specs=specs,
            scratch_shapes=[spread],
            input_output_aliases={len(operands) + i: i for i in range(len(held))},
            cost_estimate=cost(rows),
            compiler_params=params(8),
        )(*operands, *map(in_vmem, held))

    def send(array, pairs):
        return in_vmem(lax.ppermute(array, "gx", pairs))

    parts = row_parts(height)
    offs = []
    for start, rows in parts:
        (off,) = step_one(start, rows, (OFF,))
        offs.append(send(off, off_pairs))
    on, flat = step_one(0, height, (ON, STILL))
    on = send(on, on_pairs)
    arrived, carried = [], ()
    for p, part in enumerate(parts):
        (off,) = step_two([part], (OFF,), [offs[p]], on, flat)
        arrived.append(send(off, off_pairs))
        carried = step_two([part], (ON, STILL), [offs[p]], on, flat, carried)
    on, flat = carried
    on, offs = send(on, on_pairs), arrived

    def place(kernel, groups, result, moved, copies):
        operands = tuple(groups) + ((result,) if result is not None else ())
        return pl.pallas_call(
            kernel,
            out_shape=whole,
            in_specs=[local] * len(groups) + [anywhere] * (result is not None),
            out_specs=anywhere,
            scratch_shapes=[pltpu.VMEM(moved, f32), pltpu.SemaphoreType.DMA((copies,))],
            input_output_aliases={len(groups): 0} if result is not None else {},
            cost_estimate=pl.CostEstimate(
                flops=0, bytes_accessed=20 * height * breadth, transcendentals=0
            ),
            compiler_params=params(4),
        )(*operands)

    result = place(place_flat_kernel, [flat], None, (9, height, breadth), 9)
    for p, (start, rows) in enumerate(parts):
        if p == len(parts) - 1:
            result = place(place_on_kernel, [on], result, (5, height, breadth), 5)
        kernel = functools.partial(place_off_kernel, p, start, height)
        moved = (2, rows + 2 * ROWS, breadth)
        result = place(kernel, offs[: p + 1], result, moved, 6)
    return result.reshape(channels, depth, height, breadth)


def solution(mesh):
    in_specs = (P(None, ("sample", "gx"), None, None), P(("sample", "gx"), None, None), P(), P())
    out_specs = P(None, ("sample", "gx"), None, None)
    return jax.shard_map(
        on_device, mesh=mesh, in_specs=in_specs, out_specs=out_specs, check_vma=False
    )
```

```python
import functools

import jax
import jax.numpy as jnp
import numpy as np
from jax import lax
from jax.experimental import pallas as pl
from jax.experimental.pallas import tpu as pltpu
from jax.sharding import PartitionSpec as P

EIGHTHS = (4, 4)
COEFFICIENTS = 52
GROUPS = (0, 1, 3, 6, 10)
LANES = 128
ROWS = 8

UP = (1, 7, 9, 11, 13)
DOWN = (2, 10, 8, 14, 12)
GROUP_SHIFTS = ((0, 0), (1, 0), (-1, 0), (0, 1), (0, -1))
BOUNCE = (0, 2, 1, 4, 3)
FLAT = (0, 3, 4, 5, 6, 15, 16, 17, 18)
FLAT_SHIFTS = ((0, 0), (1, 0), (-1, 0), (0, 1), (0, -1), (1, 1), (-1, -1), (1, -1), (-1, 1))
FLAT_OPPOSITE = (0, 2, 1, 4, 3, 6, 5, 8, 7)


def moment_tables():
    velocities = np.array(
        [
            [0, 0, 0],
            [1, 0, 0],
            [-1, 0, 0],
            [0, 1, 0],
            [0, -1, 0],
            [0, 0, 1],
            [0, 0, -1],
            [1, 1, 0],
            [-1, -1, 0],
            [1, -1, 0],
            [-1, 1, 0],
            [1, 0, 1],
            [-1, 0, -1],
            [1, 0, -1],
            [-1, 0, 1],
            [0, 1, 1],
            [0, -1, -1],
            [0, 1, -1],
            [0, -1, 1],
        ]
    )
    x, y, z = velocities.T
    polynomials = np.stack(
        [
            np.ones(19),
            x,
            y,
            z,
            x * y,
            x * z,
            y * z,
            x**2,
            y**2,
            z**2,
            x * y**2,
            x * z**2,
            x**2 * y,
            x**2 * z,
            y * z**2,
            y**2 * z,
            x**2 * y**2,
            x**2 * z**2,
            y**2 * z**2,
        ]
    ).astype(np.float64)
    basis = []
    for row in polynomials:
        vector = row.copy()
        for earlier in basis:
            vector = vector - vector @ earlier / (earlier @ earlier) * earlier
        basis.append(vector)
    moments = np.stack(basis)
    classes = ((0, 7, 8, 9, 16, 17, 18), (1, 10, 11), (2, 12, 14), (3, 13, 15))
    tables = []
    for numbers in classes:
        rows = list(numbers)
        lower = moments[rows] @ np.linalg.pinv(polynomials[rows])
        lower = np.where(np.abs(lower) < 1e-12, 0.0, lower)
        inverse = np.linalg.inv(lower)
        inverse = np.where(np.abs(inverse) < 1e-12, 0.0, inverse)
        tables.append((numbers, lower, inverse))
    return tables


def relaxing_entries(rates):
    matrices = []
    for numbers, lower, inverse in moment_tables():
        size = len(numbers)
        matrix = {}
        for i in range(size):
            for j in range(i + 1):
                total = None
                for m in range(j, i + 1):
                    factor = float(inverse[i, m] * lower[m, j])
                    if factor == 0.0:
                        continue
                    term = rates[numbers[m]] * factor
                    total = term if total is None else total + term
                if total is not None:
                    matrix[i, j] = total * 0.5 if i or size == 3 else total
        matrices.append(matrix)
    return matrices


def apply_lower(matrix, vector):
    out = []
    for i in range(len(vector)):
        total = None
        for j in range(i + 1):
            if (i, j) in matrix:
                term = matrix[i, j]() * vector[j]
                total = term if total is None else total + term
        out.append(total)
    return out


def relax(ahead, back, flat, solid, matrices, cross_rates, push):
    def butterfly(pp, pm, mp, mm):
        a, b, c, d = pp + pm, pp - pm, mp + mm, mp - mm
        return a + c, a - c, b + d, b - d

    sx, sy, sz = ahead[0] + back[0], flat[1] + flat[2], flat[3] + flat[4]
    xy, xy_x, xy_y, xy_xy = butterfly(ahead[1], ahead[2], back[1], back[2])
    xz, xz_x, xz_z, xz_xz = butterfly(ahead[3], ahead[4], back[3], back[4])
    yz, yz_y, yz_z, yz_yz = butterfly(flat[5], flat[7], flat[8], flat[6])
    density = (flat[0] + (sx + sy)) + ((sz + xy) + (xz + yz))
    jx = (ahead[0] - back[0]) + (xy_x + xz_x)
    jy = (flat[1] - flat[2]) + (xy_y + yz_y)
    jz = (flat[3] - flat[4]) + (xz_z + yz_z)
    over = 1.0 / density
    ux, uy, uz = jx * over, jy * over, jz * over
    qxx, qyy, qzz = jx * ux, jy * uy, jz * uz
    energy = 1.5 * (qxx + (qyy + qzz))
    still = density - energy
    base = still * (1.0 / 9.0)
    hx, hy, hz = 0.5 * qxx, 0.5 * qyy, 0.5 * qzz
    bx, by, bz = base + hx, base + hy, base + hz
    xy, xz, yz = xy - (bx + hy), xz - (bx + hz), yz - (by + hz)
    raw = [
        density - (still + energy),
        (sx - bx) + (xy + xz),
        (sy - by) + (xy + yz),
        (sz - bz) + (xz + yz),
        xy,
        xz,
        yz,
    ]
    total, mx, my, mz, cxy, cxz, cyz = apply_lower(matrices[0], raw)
    even_x, even_y, even_z = mx - (cxy + cxz), my - (cxy + cyz), mz - (cxz + cyz)
    rest = (mx + my) + ((mz - cxy) - (cxz + cyz))
    even_rest = total - (rest + rest)
    even_xy, even_xz, even_yz = 0.5 * cxy, 0.5 * cxz, 0.5 * cyz

    def odd_class(matrix, current, first, second, force):
        mean = current * (1.0 / 3.0)
        departures = [current - 3.0 * mean, first - mean, second - mean]
        along, first, second = apply_lower(matrix, departures)
        lift = density * force()
        along = along - (lift + (first + second))
        return along, 0.5 * (first - lift), 0.5 * (second - lift)

    odd_x, odd_xy_x, odd_xz_x = odd_class(matrices[1], jx, xy_x, xz_x, push[0])
    odd_y, odd_xy_y, odd_yz_y = odd_class(matrices[2], jy, xy_y, yz_y, push[1])
    odd_z, odd_xz_z, odd_yz_z = odd_class(matrices[3], jz, xz_z, yz_z, push[2])
    both_xy = (xy_xy - jx * uy) * cross_rates[0]()
    both_xz = (xz_xz - jx * uz) * cross_rates[1]()
    both_yz = (yz_yz - jy * uz) * cross_rates[2]()

    def spread(even, first, second, both):
        a, b, c, d = even + first, second + both, even - first, second - both
        return a + b, a - b, c + d, c - d

    xy_pp, xy_pm, xy_mp, xy_mm = spread(even_xy, odd_xy_x, odd_xy_y, both_xy)
    xz_pp, xz_pm, xz_mp, xz_mm = spread(even_xz, odd_xz_x, odd_xz_z, both_xz)
    yz_pp, yz_pm, yz_mp, yz_mm = spread(even_yz, odd_yz_y, odd_yz_z, both_yz)
    new_ahead = [even_x + odd_x, xy_pp, xy_pm, xz_pp, xz_pm]
    new_back = [even_x - odd_x, xy_mp, xy_mm, xz_mp, xz_mm]
    new_flat = [
        even_rest,
        even_y + odd_y,
        even_y - odd_y,
        even_z + odd_z,
        even_z - odd_z,
        yz_pp,
        yz_mm,
        yz_pm,
        yz_mp,
    ]
    out_ahead = [
        jnp.where(solid, back[BOUNCE[k]], ahead[k] - new_ahead[k]) for k in range(5)
    ]
    out_back = [jnp.where(solid, ahead[BOUNCE[k]], back[k] - new_back[k]) for k in range(5)]
    out_flat = [
        jnp.where(solid, flat[FLAT_OPPOSITE[k]], flat[k] - new_flat[k]) for k in range(9)
    ]
    return out_ahead, out_back, out_flat


def local_frame():
    return lax.rem(lax.axis_index("gx"), 2)


def select_channel(side, k):
    return jnp.where(side == 1, UP[k], DOWN[k])


def scalars(rates_ref, force_ref, side, spread):
    rates = [rates_ref[m] for m in range(19)]
    sixth = 1.0 / 6.0
    sign = jnp.where(side == 1, sixth, -sixth).astype(jnp.float32)
    push = (force_ref[0] * sign, force_ref[1] * sixth, force_ref[2] * sixth)
    cross = tuple(rates[m] * 0.25 for m in (4, 5, 6))
    slots = iter(range(spread.shape[0]))

    def kept(value):
        slot = next(slots)
        spread[slot] = jnp.full(spread.shape[1:], value, jnp.float32)
        return lambda: spread[slot]

    matrices = [
        {place: kept(value) for place, value in matrix.items()}
        for matrix in relaxing_entries(rates)
    ]
    return matrices, tuple(map(kept, cross)), tuple(map(kept, push))


def shift_in_z(halves, step):
    if step == 0:
        return halves
    lane = lax.broadcasted_iota(jnp.int32, halves[0].shape, 1)
    edge = lane == (0 if step > 0 else LANES - 1)
    low, high = (pltpu.roll(value, step % LANES, 1) for value in halves)
    return jnp.where(edge, high, low), jnp.where(edge, low, high)


def relax_tile(load, solid_ref, solid_row, coefficients):
    halves = []
    for lane in range(0, solid_ref.shape[1], LANES):
        solid = solid_ref[pl.ds(solid_row, ROWS), pl.ds(lane, LANES)] == 1
        ahead, back, flat = relax(*load(lane), solid, *coefficients)
        halves.append(ahead + back + flat)
    return list(zip(*halves, strict=True))


OFF, ON, STILL = "off", "on", "still"
GROUP_SIZE = {OFF: 5, ON: 5, STILL: 9}


def wanted(groups, refs):
    first = {OFF: 0, ON: 5, STILL: 10}
    shifts = {OFF: GROUP_SHIFTS, ON: GROUP_SHIFTS, STILL: FLAT_SHIFTS}
    return [
        (first[group] + k, ref, k, shifts[group][k])
        for group, ref in zip(groups, refs, strict=True)
        for k in range(GROUP_SIZE[group])
    ]


def first_kernel(start, rows, groups, f_ref, mask_ref, rates_hbm, force_hbm, *refs):
    *results, f, solid, out, spread, rates, force, sems = refs
    height = mask_ref.shape[0]
    tiles = rows // ROWS + 2
    targets = wanted(groups, results)
    closed = rows == height
    collided = range(1, tiles - 1) if closed else range(tiles)
    copied = {1: tiles - 1, tiles - 2: 0} if closed else {}

    def fetch(i):
        row = (start + (i - 1) * ROWS) % height
        return pltpu.make_async_copy(
            f_ref.at[:, pl.ds(row, ROWS), :], f.at[:, pl.ds(i * ROWS, ROWS), :], sems.at[i]
        )

    small = [
        pltpu.make_async_copy(rates_hbm, rates, sems.at[tiles]),
        pltpu.make_async_copy(force_hbm, force, sems.at[tiles + 1]),
        pltpu.make_async_copy(mask_ref, solid, sems.at[tiles + 2]),
    ]
    for copy in small[:2]:
        copy.start()
    for i in collided:
        fetch(i).start()
        if i == 1:
            small[2].start()
    side = local_frame()
    toward = [select_channel(side, k) for k in range(5)]
    away = [select_channel(1 - side, k) for k in range(5)]
    channels = toward + away + list(FLAT)
    for copy in small[:2]:
        copy.wait()
    coefficients = scalars(rates, force, side, spread)

    def collide(i):
        local = i * ROWS
        if i in GROUPS:
            end = min((g for g in GROUPS if g > i), default=tiles)
            for j in range(i, min(end, collided[-1] + 1)):
                fetch(j).wait()
        if i == collided[0]:
            small[2].wait()

        def load(lane):
            values = [f[c, pl.ds(local, ROWS), pl.ds(lane, LANES)] for c in channels]
            return values[:5], values[5:10], values[10:]

        row = (start + (i - 1) * ROWS) % height
        pairs = relax_tile(load, solid, row, coefficients)
        for slot, (place, *_) in enumerate(targets):
            for half in range(2):
                out[slot, half, pl.ds(local, ROWS), :] = pairs[place][half]
                if i in copied:
                    out[slot, half, pl.ds(copied[i] * ROWS, ROWS), :] = pairs[place][half]

    def emit(i):
        local = i * ROWS
        row = local - ROWS
        for slot, (_, ref, entry, (step_y, step_z)) in enumerate(targets):
            pair = tuple(out[slot, half, pl.ds(local - step_y, ROWS), :] for half in range(2))
            pair = shift_in_z(pair, step_z)
            for half in range(2):
                ref[entry, pl.ds(row, ROWS), pl.ds(half * LANES, LANES)] = pair[half]

    for i in collided:
        collide(i)
        if i >= collided[0] + 2:
            emit(i - 1)
    if closed:
        emit(tiles - 2)
        emit(1)


def second_kernel(parts, groups, begin, *refs):
    off_in, refs = refs[: len(parts)], refs[len(parts) :]
    on_in, flat_in, solid, rates, force, *results, spread = refs
    results = results[-len(groups) :]
    coefficients = scalars(rates, force, local_frame(), spread)
    targets = wanted(groups, results)
    for (start, rows), arrived in zip(parts, off_in, strict=True):
        for local in range(0, rows, ROWS):

            def load(lane, local=local, start=start, arrived=arrived):
                own = (pl.ds(local, ROWS), pl.ds(lane, LANES))
                where = (pl.ds(start + local, ROWS), pl.ds(lane, LANES))
                return (
                    [on_in[(k, *where)] for k in range(5)],
                    [arrived[(k, *own)] for k in range(5)],
                    [flat_in[(k, *where)] for k in range(9)],
                )

            pairs = relax_tile(load, solid, start + local, coefficients)
            for place, ref, entry, (_, step_z) in targets:
                pair = shift_in_z(pairs[place], step_z)
                for half in range(2):
                    ref[entry, pl.ds(start - begin + local, ROWS), pl.ds(half * LANES, LANES)] = pair[half]


def place_all(refs, out_ref, moved, sems, number_of, shifts):
    copies = []
    for k, (step, _) in enumerate(shifts):
        both = jnp.concatenate([ref[k] for ref in refs], axis=0)
        moved[k] = pltpu.roll(both, step % both.shape[0], 0) if step else both
        copies.append(pltpu.make_async_copy(moved.at[k], out_ref.at[number_of(k)], sems.at[k]))
        copies[-1].start()
    for copy in copies:
        copy.wait()


def place_flat_kernel(*refs):
    *parts, out_ref, moved, sems = refs
    place_all(parts, out_ref, moved, sems, lambda k: FLAT[k], FLAT_SHIFTS)


def place_on_kernel(*refs):
    *parts, _, out_ref, moved, sems = refs
    side = local_frame()
    place_all(parts, out_ref, moved, sems, lambda k: select_channel(side, k), GROUP_SHIFTS)


def place_off_kernel(p, start, height, *refs):
    *parts, _, out_ref, moved, sems = refs
    side = local_frame()
    own = parts[p]
    rows = own.shape[1]
    first, last = p == 0, start + rows == height
    copies = []

    def send(source, k, to, slot):
        copies.append(
            pltpu.make_async_copy(
                source, out_ref.at[select_channel(1 - side, k), pl.ds(to, source.shape[0]), :], sems.at[slot]
            )
        )
        copies[-1].start()

    slot = 3
    for entry, k in enumerate((1, 2)):
        step = GROUP_SHIFTS[k][0]
        stack = [own[k]]
        if not first:
            stack.insert(0, parts[p - 1][k, pl.ds(parts[p - 1].shape[1] - ROWS, ROWS), :])
        if last:
            stack.append(parts[0][k, pl.ds(0, ROWS), :])
        stack = jnp.concatenate(stack, axis=0)
        size = stack.shape[0]
        moved[entry, pl.ds(0, size), :] = pltpu.roll(stack, step % size, 0)
        begin = start - (0 if first else ROWS)
        low = ROWS if step > 0 else 0
        high = size - (ROWS if step < 0 else 0)
        if last and step > 0:
            send(moved.at[entry, pl.ds(high - ROWS, ROWS), :], k, 0, slot)
            slot += 1
            high -= ROWS
        send(moved.at[entry, pl.ds(low, high - low), :], k, begin + low, slot)
        slot += 1
    for slot, k in enumerate((0, 3, 4)):
        send(own.at[k], k, start, slot)
    for copy in copies:
        copy.wait()


def in_vmem(array):
    return pltpu.with_memory_space_constraint(array, pltpu.VMEM)


def in_hbm(array):
    return pltpu.with_memory_space_constraint(array, pltpu.HBM)


def vmem_result(shape):
    return pltpu.VMEM(shape, jnp.float32)


def hbm_result(shape):
    return pltpu.HBM(shape, jnp.float32)


def params(mebibytes):
    return pltpu.CompilerParams(vmem_limit_bytes=mebibytes << 20)


def in_smem(array):
    return pltpu.with_memory_space_constraint(array, pltpu.SMEM)


def row_parts(height):
    sizes = [height * eighths // 8 for eighths in EIGHTHS]
    assert all(size % ROWS == 0 for size in sizes) and sum(sizes) == height
    return [(sum(sizes[:p]), size) for p, size in enumerate(sizes)]


def on_device(populations, solid_mask, relax_rates, body_force):
    channels, depth, height, breadth = populations.shape
    assert depth == 1 and breadth == 2 * LANES
    count = lax.axis_size("gx")
    assert count % 2 == 0
    off_pairs = [(i, (i + 1) % count if i % 2 else (i - 1) % count) for i in range(count)]
    on_pairs = [(i, i ^ 1) for i in range(count)]
    plane = in_hbm(populations.reshape(channels, height, breadth))
    mask = solid_mask.reshape(height, breadth)
    f32 = jnp.float32
    anywhere = pl.BlockSpec(memory_space=pl.ANY)
    local = pl.BlockSpec(memory_space=pltpu.VMEM)
    small = pl.BlockSpec(memory_space=pltpu.SMEM)
    whole = hbm_result((channels, height, breadth))
    spread = pltpu.VMEM((COEFFICIENTS, ROWS, LANES), f32)

    def cost(rows):
        nodes = rows * breadth
        return pl.CostEstimate(flops=320 * nodes, bytes_accessed=160 * nodes, transcendentals=0)

    def results(groups, rows):
        shapes = tuple(vmem_result((GROUP_SIZE[group], rows, breadth)) for group in groups)
        return shapes, tuple(local for _ in shapes)

    def step_one(start, rows, groups):
        tiles = rows // ROWS + 2
        shapes, specs = results(groups, rows)
        kept = sum(GROUP_SIZE[group] for group in groups)
        return pl.pallas_call(
            functools.partial(first_kernel, start, rows, groups),
            out_shape=shapes,
            in_specs=[anywhere] * 4,
            out_specs=specs,
            scratch_shapes=[
                pltpu.VMEM((channels, tiles * ROWS, breadth), f32),
                pltpu.VMEM((height, breadth), jnp.int32),
                pltpu.VMEM((kept, 2, tiles * ROWS, LANES), f32),
                spread,
                pltpu.SMEM(relax_rates.shape, f32),
                pltpu.SMEM(body_force.shape, f32),
                pltpu.SemaphoreType.DMA((tiles + 3,)),
            ],
            cost_estimate=cost(rows),
            compiler_params=params(8),
        )(plane, in_hbm(mask), in_hbm(relax_rates), in_hbm(body_force))

    def step_two(parts, groups, off, on, flat, carried=None):
        rows = height if carried is not None else sum(rows for _, rows in parts)
        begin = 0 if carried is not None else parts[0][0]
        shapes, specs = results(groups, rows)
        operands = (*off, on, flat, in_vmem(mask), in_smem(relax_rates), in_smem(body_force))
        held = tuple(carried or ())
        return pl.pallas_call(
            functools.partial(second_kernel, parts, groups, begin),
            out_shape=shapes,
            in_specs=[local] * (len(parts) + 3) + [small, small] + [local] * len(held),
            out_specs=specs,
            scratch_shapes=[spread],
            input_output_aliases={len(operands) + i: i for i in range(len(held))},
            cost_estimate=cost(rows),
            compiler_params=params(8),
        )(*operands, *map(in_vmem, held))

    def send(array, pairs):
        return in_vmem(lax.ppermute(array, "gx", pairs))

    parts = row_parts(height)
    offs = []
    for start, rows in parts:
        (off,) = step_one(start, rows, (OFF,))
        offs.append(send(off, off_pairs))
    on, flat = step_one(0, height, (ON, STILL))
    on = send(on, on_pairs)
    arrived, carried = [], ()
    for p, part in enumerate(parts):
        (off,) = step_two([part], (OFF,), [offs[p]], on, flat)
        arrived.append(send(off, off_pairs))
        carried = step_two([part], (ON, STILL), [offs[p]], on, flat, carried)
    on, flat = carried
    on, offs = send(on, on_pairs), arrived

    def place(kernel, groups, result, moved, copies):
        operands = tuple(groups) + ((result,) if result is not None else ())
        return pl.pallas_call(
            kernel,
            out_shape=whole,
            in_specs=[local] * len(groups) + [anywhere] * (result is not None),
            out_specs=anywhere,
            scratch_shapes=[pltpu.VMEM(moved, f32), pltpu.SemaphoreType.DMA((copies,))],
            input_output_aliases={len(groups): 0} if result is not None else {},
            cost_estimate=pl.CostEstimate(
                flops=0, bytes_accessed=20 * height * breadth, transcendentals=0
            ),
            compiler_params=params(4),
        )(*operands)

    result = place(place_flat_kernel, [flat], None, (9, height, breadth), 9)
    for p, (start, rows) in enumerate(parts):
        if p == len(parts) - 1:
            result = place(place_on_kernel, [on], result, (5, height, breadth), 5)
        kernel = functools.partial(place_off_kernel, p, start, height)
        moved = (2, rows + 2 * ROWS, breadth)
        result = place(kernel, offs[: p + 1], result, moved, 6)
    return result.reshape(channels, depth, height, breadth)


def solution(mesh):
    in_specs = (P(None, ("sample", "gx"), None, None), P(("sample", "gx"), None, None), P(), P())
    out_specs = P(None, ("sample", "gx"), None, None)
    return jax.shard_map(
        on_device, mesh=mesh, in_specs=in_specs, out_specs=out_specs, check_vma=False
    )
```

```python
import functools

import jax
import jax.numpy as jnp
import numpy as np
from jax import lax
from jax.experimental import pallas as pl
from jax.experimental.pallas import tpu as pltpu
from jax.sharding import PartitionSpec as P

EIGHTHS = (4, 4)
COEFFICIENTS = 52
GROUPS = (0, 1, 3, 6, 10)
LANES = 128
ROWS = 8

UP = (1, 7, 9, 11, 13)
DOWN = (2, 10, 8, 14, 12)
GROUP_SHIFTS = ((0, 0), (1, 0), (-1, 0), (0, 1), (0, -1))
BOUNCE = (0, 2, 1, 4, 3)
FLAT = (0, 3, 4, 5, 6, 15, 16, 17, 18)
FLAT_SHIFTS = ((0, 0), (1, 0), (-1, 0), (0, 1), (0, -1), (1, 1), (-1, -1), (1, -1), (-1, 1))
FLAT_OPPOSITE = (0, 2, 1, 4, 3, 6, 5, 8, 7)


def moment_tables():
    velocities = np.array(
        [
            [0, 0, 0],
            [1, 0, 0],
            [-1, 0, 0],
            [0, 1, 0],
            [0, -1, 0],
            [0, 0, 1],
            [0, 0, -1],
            [1, 1, 0],
            [-1, -1, 0],
            [1, -1, 0],
            [-1, 1, 0],
            [1, 0, 1],
            [-1, 0, -1],
            [1, 0, -1],
            [-1, 0, 1],
            [0, 1, 1],
            [0, -1, -1],
            [0, 1, -1],
            [0, -1, 1],
        ]
    )
    x, y, z = velocities.T
    polynomials = np.stack(
        [
            np.ones(19),
            x,
            y,
            z,
            x * y,
            x * z,
            y * z,
            x**2,
            y**2,
            z**2,
            x * y**2,
            x * z**2,
            x**2 * y,
            x**2 * z,
            y * z**2,
            y**2 * z,
            x**2 * y**2,
            x**2 * z**2,
            y**2 * z**2,
        ]
    ).astype(np.float64)
    basis = []
    for row in polynomials:
        vector = row.copy()
        for earlier in basis:
            vector = vector - vector @ earlier / (earlier @ earlier) * earlier
        basis.append(vector)
    moments = np.stack(basis)
    classes = ((0, 7, 8, 9, 16, 17, 18), (1, 10, 11), (2, 12, 14), (3, 13, 15))
    tables = []
    for numbers in classes:
        rows = list(numbers)
        lower = moments[rows] @ np.linalg.pinv(polynomials[rows])
        lower = np.where(np.abs(lower) < 1e-12, 0.0, lower)
        inverse = np.linalg.inv(lower)
        inverse = np.where(np.abs(inverse) < 1e-12, 0.0, inverse)
        tables.append((numbers, lower, inverse))
    return tables


def relaxing_entries(rates):
    matrices = []
    for numbers, lower, inverse in moment_tables():
        size = len(numbers)
        matrix = {}
        for i in range(size):
            for j in range(i + 1):
                total = None
                for m in range(j, i + 1):
                    factor = float(inverse[i, m] * lower[m, j])
                    if factor == 0.0:
                        continue
                    term = rates[numbers[m]] * factor
                    total = term if total is None else total + term
                if total is not None:
                    matrix[i, j] = total * 0.5 if i or size == 3 else total
        matrices.append(matrix)
    return matrices


def apply_lower(matrix, vector):
    out = []
    for i in range(len(vector)):
        total = None
        for j in range(i + 1):
            if (i, j) in matrix:
                term = matrix[i, j]() * vector[j]
                total = term if total is None else total + term
        out.append(total)
    return out


def relax(ahead, back, flat, solid, matrices, cross_rates, push):
    def butterfly(pp, pm, mp, mm):
        a, b, c, d = pp + pm, pp - pm, mp + mm, mp - mm
        return a + c, a - c, b + d, b - d

    sx, sy, sz = ahead[0] + back[0], flat[1] + flat[2], flat[3] + flat[4]
    xy, xy_x, xy_y, xy_xy = butterfly(ahead[1], ahead[2], back[1], back[2])
    xz, xz_x, xz_z, xz_xz = butterfly(ahead[3], ahead[4], back[3], back[4])
    yz, yz_y, yz_z, yz_yz = butterfly(flat[5], flat[7], flat[8], flat[6])
    density = (flat[0] + (sx + sy)) + ((sz + xy) + (xz + yz))
    jx = (ahead[0] - back[0]) + (xy_x + xz_x)
    jy = (flat[1] - flat[2]) + (xy_y + yz_y)
    jz = (flat[3] - flat[4]) + (xz_z + yz_z)
    over = 1.0 / density
    ux, uy, uz = jx * over, jy * over, jz * over
    qxx, qyy, qzz = jx * ux, jy * uy, jz * uz
    energy = 1.5 * (qxx + (qyy + qzz))
    still = density - energy
    base = still * (1.0 / 9.0)
    hx, hy, hz = 0.5 * qxx, 0.5 * qyy, 0.5 * qzz
    bx, by, bz = base + hx, base + hy, base + hz
    xy, xz, yz = xy - (bx + hy), xz - (bx + hz), yz - (by + hz)
    raw = [
        density - (still + energy),
        (sx - bx) + (xy + xz),
        (sy - by) + (xy + yz),
        (sz - bz) + (xz + yz),
        xy,
        xz,
        yz,
    ]
    total, mx, my, mz, cxy, cxz, cyz = apply_lower(matrices[0], raw)
    even_x, even_y, even_z = mx - (cxy + cxz), my - (cxy + cyz), mz - (cxz + cyz)
    rest = (mx + my) + ((mz - cxy) - (cxz + cyz))
    even_rest = total - (rest + rest)
    even_xy, even_xz, even_yz = 0.5 * cxy, 0.5 * cxz, 0.5 * cyz

    def odd_class(matrix, current, first, second, force):
        mean = current * (1.0 / 3.0)
        departures = [current - 3.0 * mean, first - mean, second - mean]
        along, first, second = apply_lower(matrix, departures)
        lift = density * force()
        along = along - (lift + (first + second))
        return along, 0.5 * (first - lift), 0.5 * (second - lift)

    odd_x, odd_xy_x, odd_xz_x = odd_class(matrices[1], jx, xy_x, xz_x, push[0])
    odd_y, odd_xy_y, odd_yz_y = odd_class(matrices[2], jy, xy_y, yz_y, push[1])
    odd_z, odd_xz_z, odd_yz_z = odd_class(matrices[3], jz, xz_z, yz_z, push[2])
    both_xy = (xy_xy - jx * uy) * cross_rates[0]()
    both_xz = (xz_xz - jx * uz) * cross_rates[1]()
    both_yz = (yz_yz - jy * uz) * cross_rates[2]()

    def spread(even, first, second, both):
        a, b, c, d = even + first, second + both, even - first, second - both
        return a + b, a - b, c + d, c - d

    xy_pp, xy_pm, xy_mp, xy_mm = spread(even_xy, odd_xy_x, odd_xy_y, both_xy)
    xz_pp, xz_pm, xz_mp, xz_mm = spread(even_xz, odd_xz_x, odd_xz_z, both_xz)
    yz_pp, yz_pm, yz_mp, yz_mm = spread(even_yz, odd_yz_y, odd_yz_z, both_yz)
    new_ahead = [even_x + odd_x, xy_pp, xy_pm, xz_pp, xz_pm]
    new_back = [even_x - odd_x, xy_mp, xy_mm, xz_mp, xz_mm]
    new_flat = [
        even_rest,
        even_y + odd_y,
        even_y - odd_y,
        even_z + odd_z,
        even_z - odd_z,
        yz_pp,
        yz_mm,
        yz_pm,
        yz_mp,
    ]
    out_ahead = [
        jnp.where(solid, back[BOUNCE[k]], ahead[k] - new_ahead[k]) for k in range(5)
    ]
    out_back = [jnp.where(solid, ahead[BOUNCE[k]], back[k] - new_back[k]) for k in range(5)]
    out_flat = [
        jnp.where(solid, flat[FLAT_OPPOSITE[k]], flat[k] - new_flat[k]) for k in range(9)
    ]
    return out_ahead, out_back, out_flat


def local_frame():
    return lax.rem(lax.axis_index("gx"), 2)


def select_channel(side, k):
    return jnp.where(side == 1, UP[k], DOWN[k])


def scalars(rates_ref, force_ref, side, spread):
    rates = [rates_ref[m] for m in range(19)]
    sixth = 1.0 / 6.0
    sign = jnp.where(side == 1, sixth, -sixth).astype(jnp.float32)
    push = (force_ref[0] * sign, force_ref[1] * sixth, force_ref[2] * sixth)
    cross = tuple(rates[m] * 0.25 for m in (4, 5, 6))
    slots = iter(range(spread.shape[0]))

    def kept(value):
        slot = next(slots)
        spread[slot] = jnp.full(spread.shape[1:], value, jnp.float32)
        return lambda: spread[slot]

    matrices = [
        {place: kept(value) for place, value in matrix.items()}
        for matrix in relaxing_entries(rates)
    ]
    return matrices, tuple(map(kept, cross)), tuple(map(kept, push))


def kept_scalars(spread):
    slots = iter(range(spread.shape[0]))

    def kept():
        slot = next(slots)
        return lambda: spread[slot]

    matrices = [{place: kept() for place in matrix} for matrix in relaxing_entries([1.0] * 19)]
    return matrices, tuple(kept() for _ in range(3)), tuple(kept() for _ in range(3))


def shift_in_z(halves, step):
    if step == 0:
        return halves
    lane = lax.broadcasted_iota(jnp.int32, halves[0].shape, 1)
    edge = lane == (0 if step > 0 else LANES - 1)
    low, high = (pltpu.roll(value, step % LANES, 1) for value in halves)
    return jnp.where(edge, high, low), jnp.where(edge, low, high)


def relax_tile(load, solid_ref, solid_row, coefficients):
    halves = []
    for lane in range(0, solid_ref.shape[1], LANES):
        solid = solid_ref[pl.ds(solid_row, ROWS), pl.ds(lane, LANES)] == 1
        ahead, back, flat = relax(*load(lane), solid, *coefficients)
        halves.append(ahead + back + flat)
    return list(zip(*halves, strict=True))


OFF, ON, STILL = "off", "on", "still"
GROUP_SIZE = {OFF: 5, ON: 5, STILL: 9}


def wanted(groups, refs):
    first = {OFF: 0, ON: 5, STILL: 10}
    shifts = {OFF: GROUP_SHIFTS, ON: GROUP_SHIFTS, STILL: FLAT_SHIFTS}
    return [
        (first[group] + k, ref, k, shifts[group][k])
        for group, ref in zip(groups, refs, strict=True)
        for k in range(GROUP_SIZE[group])
    ]


def first_kernel(start, rows, groups, share, f_ref, mask_ref, rates_hbm, force_hbm, *refs):
    if share:
        *results, spread, f, solid, out, rates, force, sems = refs
    else:
        *results, f, solid, out, spread, rates, force, sems = refs
    height = mask_ref.shape[0]
    tiles = rows // ROWS + 2
    targets = wanted(groups, results)
    closed = rows == height
    collided = range(1, tiles - 1) if closed else range(tiles)
    copied = {1: tiles - 1, tiles - 2: 0} if closed else {}

    def fetch(i):
        row = (start + (i - 1) * ROWS) % height
        return pltpu.make_async_copy(
            f_ref.at[:, pl.ds(row, ROWS), :], f.at[:, pl.ds(i * ROWS, ROWS), :], sems.at[i]
        )

    small = [
        pltpu.make_async_copy(rates_hbm, rates, sems.at[tiles]),
        pltpu.make_async_copy(force_hbm, force, sems.at[tiles + 1]),
        pltpu.make_async_copy(mask_ref, solid, sems.at[tiles + 2]),
    ]
    for copy in small[:2]:
        copy.start()
    for i in collided:
        fetch(i).start()
        if i == 1:
            small[2].start()
    side = local_frame()
    toward = [select_channel(side, k) for k in range(5)]
    away = [select_channel(1 - side, k) for k in range(5)]
    channels = toward + away + list(FLAT)
    for copy in small[:2]:
        copy.wait()
    coefficients = scalars(rates, force, side, spread)

    def collide(i):
        local = i * ROWS
        if i in GROUPS:
            end = min((g for g in GROUPS if g > i), default=tiles)
            for j in range(i, min(end, collided[-1] + 1)):
                fetch(j).wait()
        if i == collided[0]:
            small[2].wait()

        def load(lane):
            values = [f[c, pl.ds(local, ROWS), pl.ds(lane, LANES)] for c in channels]
            return values[:5], values[5:10], values[10:]

        row = (start + (i - 1) * ROWS) % height
        pairs = relax_tile(load, solid, row, coefficients)
        for slot, (place, *_) in enumerate(targets):
            for half in range(2):
                out[slot, half, pl.ds(local, ROWS), :] = pairs[place][half]
                if i in copied:
                    out[slot, half, pl.ds(copied[i] * ROWS, ROWS), :] = pairs[place][half]

    def emit(i):
        local = i * ROWS
        row = local - ROWS
        for slot, (_, ref, entry, (step_y, step_z)) in enumerate(targets):
            pair = tuple(out[slot, half, pl.ds(local - step_y, ROWS), :] for half in range(2))
            pair = shift_in_z(pair, step_z)
            for half in range(2):
                ref[entry, pl.ds(row, ROWS), pl.ds(half * LANES, LANES)] = pair[half]

    for i in collided:
        collide(i)
        if i >= collided[0] + 2:
            emit(i - 1)
    if closed:
        emit(tiles - 2)
        emit(1)


def second_kernel(parts, groups, begin, *refs):
    off_in, refs = refs[: len(parts)], refs[len(parts) :]
    on_in, flat_in, solid, spread, *results = refs
    results = results[-len(groups) :]
    coefficients = kept_scalars(spread)
    targets = wanted(groups, results)
    for (start, rows), arrived in zip(parts, off_in, strict=True):
        for local in range(0, rows, ROWS):

            def load(lane, local=local, start=start, arrived=arrived):
                own = (pl.ds(local, ROWS), pl.ds(lane, LANES))
                where = (pl.ds(start + local, ROWS), pl.ds(lane, LANES))
                return (
                    [on_in[(k, *where)] for k in range(5)],
                    [arrived[(k, *own)] for k in range(5)],
                    [flat_in[(k, *where)] for k in range(9)],
                )

            pairs = relax_tile(load, solid, start + local, coefficients)
            for place, ref, entry, (_, step_z) in targets:
                pair = shift_in_z(pairs[place], step_z)
                for half in range(2):
                    ref[entry, pl.ds(start - begin + local, ROWS), pl.ds(half * LANES, LANES)] = pair[half]


def place_all(refs, out_ref, moved, sems, number_of, shifts):
    copies = []
    for k, (step, _) in enumerate(shifts):
        both = jnp.concatenate([ref[k] for ref in refs], axis=0)
        moved[k] = pltpu.roll(both, step % both.shape[0], 0) if step else both
        copies.append(pltpu.make_async_copy(moved.at[k], out_ref.at[number_of(k)], sems.at[k]))
        copies[-1].start()
    for copy in copies:
        copy.wait()


def place_flat_kernel(*refs):
    *parts, out_ref, moved, sems = refs
    place_all(parts, out_ref, moved, sems, lambda k: FLAT[k], FLAT_SHIFTS)


def place_on_kernel(*refs):
    *parts, _, out_ref, moved, sems = refs
    side = local_frame()
    place_all(parts, out_ref, moved, sems, lambda k: select_channel(side, k), GROUP_SHIFTS)


def place_off_kernel(p, start, height, *refs):
    *parts, _, out_ref, moved, sems = refs
    side = local_frame()
    own = parts[p]
    rows = own.shape[1]
    first, last = p == 0, start + rows == height
    copies = []

    def send(source, k, to, slot):
        copies.append(
            pltpu.make_async_copy(
                source, out_ref.at[select_channel(1 - side, k), pl.ds(to, source.shape[0]), :], sems.at[slot]
            )
        )
        copies[-1].start()

    slot = 3
    for entry, k in enumerate((1, 2)):
        step = GROUP_SHIFTS[k][0]
        stack = [own[k]]
        if not first:
            stack.insert(0, parts[p - 1][k, pl.ds(parts[p - 1].shape[1] - ROWS, ROWS), :])
        if last:
            stack.append(parts[0][k, pl.ds(0, ROWS), :])
        stack = jnp.concatenate(stack, axis=0)
        size = stack.shape[0]
        moved[entry, pl.ds(0, size), :] = pltpu.roll(stack, step % size, 0)
        begin = start - (0 if first else ROWS)
        low = ROWS if step > 0 else 0
        high = size - (ROWS if step < 0 else 0)
        if last and step > 0:
            send(moved.at[entry, pl.ds(high - ROWS, ROWS), :], k, 0, slot)
            slot += 1
            high -= ROWS
        send(moved.at[entry, pl.ds(low, high - low), :], k, begin + low, slot)
        slot += 1
    for slot, k in enumerate((0, 3, 4)):
        send(own.at[k], k, start, slot)
    for copy in copies:
        copy.wait()


def in_vmem(array):
    return pltpu.with_memory_space_constraint(array, pltpu.VMEM)


def in_hbm(array):
    return pltpu.with_memory_space_constraint(array, pltpu.HBM)


def vmem_result(shape):
    return pltpu.VMEM(shape, jnp.float32)


def hbm_result(shape):
    return pltpu.HBM(shape, jnp.float32)


def params(mebibytes):
    return pltpu.CompilerParams(vmem_limit_bytes=mebibytes << 20)


def row_parts(height):
    sizes = [height * eighths // 8 for eighths in EIGHTHS]
    assert all(size % ROWS == 0 for size in sizes) and sum(sizes) == height
    return [(sum(sizes[:p]), size) for p, size in enumerate(sizes)]


def on_device(populations, solid_mask, relax_rates, body_force):
    channels, depth, height, breadth = populations.shape
    assert depth == 1 and breadth == 2 * LANES
    count = lax.axis_size("gx")
    assert count % 2 == 0
    off_pairs = [(i, (i + 1) % count if i % 2 else (i - 1) % count) for i in range(count)]
    on_pairs = [(i, i ^ 1) for i in range(count)]
    plane = in_hbm(populations.reshape(channels, height, breadth))
    mask = solid_mask.reshape(height, breadth)
    f32 = jnp.float32
    anywhere = pl.BlockSpec(memory_space=pl.ANY)
    local = pl.BlockSpec(memory_space=pltpu.VMEM)
    small = pl.BlockSpec(memory_space=pltpu.SMEM)
    whole = hbm_result((channels, height, breadth))
    spread = pltpu.VMEM((COEFFICIENTS, ROWS, LANES), f32)

    def cost(rows):
        nodes = rows * breadth
        return pl.CostEstimate(flops=320 * nodes, bytes_accessed=160 * nodes, transcendentals=0)

    def results(groups, rows):
        shapes = tuple(vmem_result((GROUP_SIZE[group], rows, breadth)) for group in groups)
        return shapes, tuple(local for _ in shapes)

    def step_one(start, rows, groups, share=False):
        tiles = rows // ROWS + 2
        shapes, specs = results(groups, rows)
        kept = sum(GROUP_SIZE[group] for group in groups)
        if share:
            shapes, specs = shapes + (vmem_result(spread.shape),), specs + (local,)
        return pl.pallas_call(
            functools.partial(first_kernel, start, rows, groups, share),
            out_shape=shapes,
            in_specs=[anywhere] * 4,
            out_specs=specs,
            scratch_shapes=[
                pltpu.VMEM((channels, tiles * ROWS, breadth), f32),
                pltpu.VMEM((height, breadth), jnp.int32),
                pltpu.VMEM((kept, 2, tiles * ROWS, LANES), f32),
                *(() if share else (spread,)),
                pltpu.SMEM(relax_rates.shape, f32),
                pltpu.SMEM(body_force.shape, f32),
                pltpu.SemaphoreType.DMA((tiles + 3,)),
            ],
            cost_estimate=cost(rows),
            compiler_params=params(8),
        )(plane, in_hbm(mask), in_hbm(relax_rates), in_hbm(body_force))

    def step_two(parts, groups, off, on, flat, carried=None):
        rows = height if carried is not None else sum(rows for _, rows in parts)
        begin = 0 if carried is not None else parts[0][0]
        shapes, specs = results(groups, rows)
        operands = (*off, on, flat, in_vmem(mask), shared)
        held = tuple(carried or ())
        return pl.pallas_call(
            functools.partial(second_kernel, parts, groups, begin),
            out_shape=shapes,
            in_specs=[local] * (len(parts) + 4 + len(held)),
            out_specs=specs,
            input_output_aliases={len(operands) + i: i for i in range(len(held))},
            cost_estimate=cost(rows),
            compiler_params=params(8),
        )(*operands, *map(in_vmem, held))

    def send(array, pairs):
        return in_vmem(lax.ppermute(array, "gx", pairs))

    parts = row_parts(height)
    offs, shared = [], None
    for p, (start, rows) in enumerate(parts):
        off, *extra = step_one(start, rows, (OFF,), share=p == 0)
        shared = extra[0] if p == 0 else shared
        offs.append(send(off, off_pairs))
    on, flat = step_one(0, height, (ON, STILL))
    on = send(on, on_pairs)
    arrived, carried = [], ()
    for p, part in enumerate(parts):
        (off,) = step_two([part], (OFF,), [offs[p]], on, flat)
        arrived.append(send(off, off_pairs))
        carried = step_two([part], (ON, STILL), [offs[p]], on, flat, carried)
    on, flat = carried
    on, offs = send(on, on_pairs), arrived

    def place(kernel, groups, result, moved, copies):
        operands = tuple(groups) + ((result,) if result is not None else ())
        return pl.pallas_call(
            kernel,
            out_shape=whole,
            in_specs=[local] * len(groups) + [anywhere] * (result is not None),
            out_specs=anywhere,
            scratch_shapes=[pltpu.VMEM(moved, f32), pltpu.SemaphoreType.DMA((copies,))],
            input_output_aliases={len(groups): 0} if result is not None else {},
            cost_estimate=pl.CostEstimate(
                flops=0, bytes_accessed=20 * height * breadth, transcendentals=0
            ),
            compiler_params=params(4),
        )(*operands)

    result = place(place_flat_kernel, [flat], None, (9, height, breadth), 9)
    for p, (start, rows) in enumerate(parts):
        if p == len(parts) - 1:
            result = place(place_on_kernel, [on], result, (5, height, breadth), 5)
        kernel = functools.partial(place_off_kernel, p, start, height)
        moved = (2, rows + 2 * ROWS, breadth)
        result = place(kernel, offs[: p + 1], result, moved, 6)
    return result.reshape(channels, depth, height, breadth)


def solution(mesh):
    in_specs = (P(None, ("sample", "gx"), None, None), P(("sample", "gx"), None, None), P(), P())
    out_specs = P(None, ("sample", "gx"), None, None)
    return jax.shard_map(
        on_device, mesh=mesh, in_specs=in_specs, out_specs=out_specs, check_vma=False
    )
```
